32 devices in a mesh: members: 2 (over y), lon: 8 (over z, x), lev: 2 (over core).
Axes of the slice: x: 2, y: 2, z: 4, core: 2. Of those that a mesh axis runs over, the one named last changes fastest.
Arguments:
- velocity: bfloat16 [2, 4, 32, 1024], P(None, ('members', 'lev'), None, 'lon'), parts along dimension 1, may hold values from -3 to 3
- land_sea: int32 [4, 32, 1024], P(('members', 'lev'), None, 'lon'), parts along dimension 0, may hold values 0 or 1
- fold_pivot: int32 [2], replicated, may hold values from 1022 to 1024, as said below
- weight_one: bfloat16 [5, 5, 2, 128], replicated, may hold values from -1.25 to 1.25
- bias_one: float32 [128], replicated, may hold values from -2 to 2
- weight_two: bfloat16 [5, 5, 128, 64], replicated, may hold values from -0.15625 to 0.15625
- bias_two: float32 [64], replicated, may hold values from -2 to 2
- weight_three: bfloat16 [3, 3, 64, 32], replicated, may hold values from -0.375 to 0.375
- bias_three: float32 [32], replicated, may hold values from -2 to 2
- weight_four: bfloat16 [3, 3, 32, 2], replicated, may hold values from -1 to 1
- bias_four: float32 [2], replicated, may hold values from -2 to 2
Outputs:
- updated: bfloat16 [2, 4, 32, 1024], P(None, ('members', 'lev'), None, 'lon'), parts along dimension 1
The draws below stay inside these ranges and needn't reach their ends.
There are 2 independent parts, one for each index of `members`. The reference program is written for one: setup_inputs(seed, part) draws one part's arguments, and reference() takes and returns one part's arrays. A program takes and returns all parts, laid end to end along the dimension named above; an argument that names none is the same for every part. Nothing has to cross between parts.
Inputs may be any that keep to these rules, and one draw needn't show every extreme that they name: `fold_pivot`: one entry is 1022 and the other 1024, in either order.
All inputs are finite; a program needn't handle non-finite values. No bound on the sum of `land_sea` on one device may be relied on, other than what follows from the above.
Results may differ from the reference program's by a relative error of at most 0.005.
The reference program's roundings to bfloat16 on the way (of `masked`, `extended`, `first`, `second` and `third`) count: a program that leaves them out, or rounds other values in their place, can miss the bound.
Values may be sent and summed in bfloat16 or wider, within the bound.
No kernel may reach another device: no remote copies, remote signals or barrier semaphores. Data moves between devices by JAX's collectives and lax.ppermute only.
A program may use at most 64 MiB of HBM per device.

```python
import jax
import jax.numpy as jnp
from jax import lax

NROW = 32
LON_DEV = 128
C1 = 128
C2 = 64
C3 = 32
NLON = 1024
LEV = 2


def draw_fold_pivot(key, part):
    flipped = jax.random.randint(jax.random.fold_in(key, 11), (), 0, 2)
    signed = 2 * flipped - 1
    return jnp.stack([NLON - 1 + signed, NLON - 1 - signed]).astype(jnp.int32)


def place_ends(drawn, stream_key, least, high):
    longest = drawn.shape.index(max(drawn.shape))
    spots = []
    for shift in (0, 1):
        where = [jax.random.randint(jax.random.fold_in(stream_key, axis), (), 0, length) for axis, length in enumerate(drawn.shape)]
        where[longest] = (where[longest] + shift) % drawn.shape[longest]
        spots.append(tuple(where))
    return drawn.at[spots[0]].set(least).at[spots[1]].set(high)


def level_of(own_key, dims, split, least, top_value):
    def one(dim, parts):
        draws = jax.random.uniform(jax.random.fold_in(jax.random.fold_in(own_key, 6), dim), (parts,), jnp.float32, least / len(split), top_value / len(split))
        return jnp.repeat(jnp.exp(draws), dims[dim] // parts).reshape((-1,) + (1,) * (len(dims) - dim - 1))

    factor_of = one(*split[0])
    for cut in split[1:]:
        factor_of = factor_of * one(*cut)
    return factor_of


def gaussian(own_key, extent, spread, reach, pieces=(), kind=jnp.bfloat16):
    drawn = spread * jax.random.normal(own_key, extent, jnp.float32)
    if pieces:
        drawn = drawn * level_of(own_key, extent, pieces, -0.22, 0.18)
    return jnp.clip(drawn, -reach, reach).astype(kind)


def setup_inputs(seed: int = 0, part: int = 0) -> dict:
    arg_keys = jax.random.split(jax.random.key(seed), 12)
    own_keys = jax.random.split(jax.random.fold_in(arg_keys[11], part), 12)
    return {
        "velocity": gaussian(own_keys[0], (2, LEV, NROW, NLON), 0.5, 3.0, ((1, 2), (3, 8))),
        "land_sea": place_ends((jax.random.randint(own_keys[1], (LEV, NROW, NLON), 0, 8) < 7).astype(jnp.int32), jax.random.fold_in(own_keys[1], 1), 0, 1),
        "fold_pivot": draw_fold_pivot(jax.random.fold_in(arg_keys[11], 71), part),
        "weight_one": gaussian(arg_keys[3], (5, 5, 2, C1), 25 ** -0.5, 1.25),
        "bias_one": gaussian(arg_keys[4], (C1,), 0.5, 2.0, (), jnp.float32),
        "weight_two": gaussian(arg_keys[5], (5, 5, C1, C2), (25 * C1 // 2) ** -0.5, 0.15625),
        "bias_two": gaussian(arg_keys[6], (C2,), 0.5, 2.0, (), jnp.float32),
        "weight_three": gaussian(arg_keys[7], (3, 3, C2, C3), (9 * C2 // 2) ** -0.5, 0.375),
        "bias_three": gaussian(arg_keys[8], (C3,), 0.5, 2.0, (), jnp.float32),
        "weight_four": gaussian(arg_keys[9], (3, 3, C3, 2), (9 * C3 // 8) ** -0.5, 1.0),
        "bias_four": gaussian(arg_keys[10], (2,), 0.5, 2.0, (), jnp.float32),
    }


def convolve(field_data, weight, bias_term):
    kernel = weight.shape[0]
    out_rows = field_data.shape[2] - kernel + 1
    out_cols = field_data.shape[3] - kernel + 1
    as_float = field_data.astype(jnp.float32)
    weight_float = weight.astype(jnp.float32)
    result = jnp.zeros((weight.shape[3], field_data.shape[1], out_rows, out_cols), jnp.float32)
    for row_shift in range(kernel):
        for col_shift in range(kernel):
            window = as_float[:, :, row_shift:row_shift + out_rows, col_shift:col_shift + out_cols]
            result = result + jnp.einsum('co,cvrl->ovrl', weight_float[row_shift, col_shift], window)
    return result + bias_term[:, None, None, None]


def reference(velocity, land_sea, fold_pivot, weight_one, bias_one, weight_two, bias_two, weight_three, bias_three, weight_four, bias_four):
    masked = velocity * land_sea.astype(jnp.bfloat16)[None]
    top_rows = masked[:, :, NROW - 7:NROW - 1, :][:, :, ::-1, :]
    columns = jnp.arange(NLON, dtype=jnp.int32)
    fold_field = jnp.stack([jnp.take(top_rows[component], ((fold_pivot[component] - columns) % NLON).astype(jnp.int32), axis=2) for component in range(2)])
    south_rows = jnp.zeros((2, LEV, 6, NLON), jnp.bfloat16)
    extended = jnp.concatenate([south_rows, masked, -fold_field], axis=2)
    padded = jnp.concatenate([extended[..., NLON - 6:], extended, extended[..., :6]], axis=3)

    def one_block(start_col):
        segment = lax.dynamic_slice_in_dim(padded, start_col.astype(jnp.int32), LON_DEV + 12, 3)
        first = jnp.maximum(convolve(segment, weight_one, bias_one), 0.0).astype(jnp.bfloat16)
        second = jnp.maximum(convolve(first, weight_two, bias_two), 0.0).astype(jnp.bfloat16)
        third = jnp.maximum(convolve(second, weight_three, bias_three), 0.0).astype(jnp.bfloat16)
        return convolve(third, weight_four, bias_four)

    starts = (jnp.arange(NLON // LON_DEV, dtype=jnp.int32) * LON_DEV).astype(jnp.int32)
    tendency = lax.map(one_block, starts)
    tendency = jnp.transpose(tendency, (1, 2, 3, 0, 4)).reshape(2, LEV, NROW, NLON)
    result = land_sea.astype(jnp.float32)[None] * (velocity.astype(jnp.float32) + tendency)
    return result.astype(jnp.bfloat16)
```

```python
import functools

import jax
import jax.numpy as jnp
from jax import lax
from jax.experimental import pallas as pl
from jax.experimental.pallas import tpu as pltpu
from jax.sharding import PartitionSpec as P

BF = jnp.bfloat16
F32 = jnp.float32
SLOT = 32
EDGE = 8


def dot(a, b):
    return jnp.dot(a, b, preferred_element_type=F32)


def dot_nt(a, b):
    return lax.dot_general(a, b, (((1,), (1,)), ((), ())), preferred_element_type=F32)


def iota(shape, dim):
    return lax.broadcasted_iota(jnp.int32, shape, dim)


def picks(pair, lanes, base, sign):
    want = lax.rem(base + sign * 2 * pair + 4 * lanes, lanes)
    return (iota(pair.shape, 1) == want).astype(BF)


def spread(patch_ref, first_row, rows, shifted):
    for tap in range(10):
        for component in range(2):
            start = first_row * SLOT + tap * 2 + component
            value = shifted(tap, component)
            for k in range(value.shape[1] // 128):
                patch_ref[k, pl.ds(start, rows, stride=SLOT), :] = value[:, 128 * k : 128 * k + 128]


def patches(patch_ref, lo, hi):
    parts = [patch_ref[k, lo:hi, :] for k in range(patch_ref.shape[0])]
    return jnp.concatenate(parts, axis=1).astype(BF)


def first_weights(w1_ref, row, half):
    lead = (w1_ref.shape[1] - 5 * SLOT) // 2
    start = lead - SLOT * row
    return jnp.concatenate(
        [w1_ref[2 * half + k, start : start + 8 * SLOT, :] for k in range(2)], axis=1
    )


def second_weights(w2_ref):
    tiles = []
    zero = jnp.zeros((256, 128), BF)
    for a in range(6):
        for half in range(3):
            part = [
                w2_ref[k, 256 * half : 256 * half + 256, :] if 0 <= k < 5 else zero
                for k in (a, a - 1)
            ]
            tiles.append(jnp.concatenate(part, axis=1))
    return jnp.concatenate(tiles, axis=0)


def body(
    pivot_ref,
    b4_ref,
    vel_ref,
    land_ref,
    own_ref,
    far_ref,
    near_a_ref,
    near_b_ref,
    w1_ref,
    b1_ref,
    w2_ref,
    b2_ref,
    w3_ref,
    b3_ref,
    w4_ref,
    out_ref,
    patch_i,
    patch_e,
    left_i,
    left_t,
    left_s,
    f_i,
    f_t,
    f_s,
    sec,
    third,
    turn,
    spill,
    tend,
    *,
    lon_count,
):
    rows = own_ref.shape[1]
    cols = own_ref.shape[2]
    bias1 = jnp.concatenate([b1_ref[...]] * 2, axis=1)
    bias2 = jnp.concatenate([b2_ref[...]] * 4, axis=1)
    bias3 = jnp.concatenate([b3_ref[...]] * 4, axis=1)
    ext_rows = rows + 12
    groups = (rows + 8) // 4
    pairs_in = (rows - 2) // 2
    groups_in = groups - 1

    own = own_ref[...].astype(F32)
    patch_i[...] = jnp.zeros_like(patch_i)
    rolled = [
        [pltpu.roll(own[c], (cols - t) % cols, axis=1) for c in range(2)] for t in range(10)
    ]
    spread(patch_i, 6, rows, lambda t, c: rolled[t][c])
    slot_pair = iota((64, cols), 0)
    pick = (iota((64, cols), 1) == 2 * slot_pair - 6).astype(BF)
    left_i[...] = dot_nt(pick, patches(patch_i, 0, ext_rows * SLOT)).astype(BF)
    stacked = jnp.concatenate(
        [left_i[:, 128 * g : 128 * g + 256] for g in range(groups_in)], axis=0
    )
    for row in range(4):
        for half in range(3):
            res = dot(stacked, first_weights(w1_ref, row, half))
            res = jnp.maximum(res + bias1, 0.0).astype(BF)
            for g in range(groups_in):
                f_i[row % 2, half, 2 * g + row // 2] = res[64 * g : 64 * g + 64]
    right2 = second_weights(w2_ref)
    step = 5
    for lo in range(0, pairs_in, step):
        left = jnp.concatenate(
            [
                f_i[a % 2, half, lo + a // 2 : lo + a // 2 + step].reshape(step * 64, 256)
                for a in range(6)
                for half in range(3)
            ],
            axis=1,
        )
        res = jnp.maximum(dot(left, right2) + bias2, 0.0)
        for k in range(step):
            sec[(lo + k) * 72 : (lo + k) * 72 + 64, :] = res[64 * k : 64 * k + 64]

    lon = lax.axis_index("lon")
    even = lax.rem(lon, 2) == 0
    own_tail = own_ref[:, rows - 8 :, :].astype(F32)
    far = far_ref[...].astype(F32)
    wrap = jnp.concatenate([far, own_tail], axis=1)
    near_a = near_a_ref[...].astype(F32)
    near_b = near_b_ref[...].astype(F32)
    west = jnp.where(lon == 0, wrap, jnp.where(even, near_b, near_a))
    east = jnp.where(lon == lon_count - 1, wrap, jnp.where(even, near_a, near_b))
    side = iota((rows, cols), 1) < cols // 2
    side8 = iota((8, cols), 1) < cols // 2
    wide = []
    fold = []
    for c in range(2):
        outer = jnp.where(side, east[c, :rows], west[c, :rows])
        wide.append(jnp.concatenate([own[c], outer], axis=1))
        outer = jnp.where(side8, west[c, rows:], east[c, rows:])
        turn[...] = jnp.concatenate([far[c, rows - 8 :], outer], axis=1)
        fold.append(
            -jnp.concatenate([turn[7 - k : 8 - k, :] for k in range(1, 7)] + [turn[0:2, :]], axis=0)
        )
    lanes = 2 * cols
    patch_e[...] = jnp.zeros_like(patch_e)
    spread(patch_e, 6, rows, lambda t, c: pltpu.roll(wide[c], (lanes - t) % lanes, axis=1))

    def folded(t, c):
        up = pivot_ref[c] - (lon_count * cols - 1) > 0
        value = jnp.where(
            up,
            pltpu.roll(fold[c], (t - 1 + lanes) % lanes, axis=1),
            pltpu.roll(fold[c], t + 1, axis=1),
        )
        return value[0:6]

    spread(patch_e, rows + 6, 6, folded)
    slot = iota((80, lanes), 0)
    strip = slot - 64
    pair = jnp.where(
        slot < 64,
        slot,
        jnp.where(strip < 3, strip, jnp.where(strip < 5, strip + 61, jnp.where(strip == 7, 63, 3))),
    )
    pick = picks(pair, lanes, -6, 1)
    pick_fold = picks(pair, lanes, cols + 5, -1)
    split = (rows + 6) * SLOT
    left = jnp.concatenate(
        [
            dot_nt(pick, patches(patch_e, 0, split)),
            dot_nt(pick_fold, patches(patch_e, split, ext_rows * SLOT)),
        ],
        axis=1,
    )
    left_t[...] = left[:64].astype(BF)
    left_s[...] = left[64:72]
    top = range(groups - 3, groups)
    stacked_t = [left_t[:, 128 * g : 128 * g + 256] for g in top]
    stacked_s = [left_s[:, 128 * g : 128 * g + 256] for g in range(groups)]
    stacked = jnp.concatenate(stacked_t + [jnp.concatenate(stacked_s, axis=0).astype(BF)], axis=0)
    for row in range(4):
        for half in range(3):
            res = dot(stacked, first_weights(w1_ref, row, half))
            res = jnp.maximum(res + bias1, 0.0)
            for g in range(3):
                f_t[row % 2, half, 2 * g + row // 2] = res[64 * g : 64 * g + 64].astype(BF)
            for g in range(groups):
                at = (2 * g + row // 2) * EDGE
                f_s[row % 2, half, at : at + EDGE, :] = res[192 + EDGE * g : 192 + EDGE * g + EDGE]
    pairs = (rows + 4) // 2
    left = jnp.concatenate(
        [
            jnp.concatenate(
                [
                    f_t[a % 2, half, 1 + a // 2 : 4 + a // 2].reshape(192, 256),
                    f_s[a % 2, half, (a // 2) * EDGE : (a // 2 + pairs) * EDGE, :].astype(BF),
                ],
                axis=0,
            )
            for a in range(6)
            for half in range(3)
        ],
        axis=1,
    )
    res = jnp.maximum(dot(left, right2) + bias2, 0.0)
    for k in range(3):
        at = (pairs - 3 + k) * 72
        sec[at : at + 64, :] = res[64 * k : 64 * k + 64]
    line = iota((EDGE, 256), 0)
    for k in range(pairs):
        new = res[192 + EDGE * k : 192 + EDGE * k + EDGE]
        at = k * 72
        sec[at : at + 8, :] = jnp.where(line < 3, new, sec[at : at + 8, :])
        sec[at + 56 : at + 64, :] = jnp.where(line == 7, new, sec[at + 56 : at + 64, :])
        sec[at + 64 : at + 72, :] = pltpu.roll(new, EDGE - 3, axis=0)

    pairs3 = pairs - 1
    size = pairs3 * 72
    left = jnp.concatenate(
        [sec[at : at + size, :].astype(BF) for at in (0, 1, 72, 73)], axis=1
    )
    third[0:size, :] = jnp.maximum(dot(left, w3_ref[...]) + bias3, 0.0)

    pairs4 = pairs - 2
    left = jnp.concatenate(
        [
            jnp.concatenate(
                [third[k * 72 + at : k * 72 + at + 64, :] for k in range(pairs4)], axis=0
            ).astype(BF)
            for at in (0, 1, 72, 73)
        ],
        axis=1,
    )
    res = dot_nt(w4_ref[...], left)
    parts = []
    for dc in range(2):
        stack = jnp.concatenate(
            [res[8 * dc : 8 * dc + 8, 128 * t : 128 * t + 128] for t in range(pairs4 // 2)], axis=0
        )
        high = stack.astype(BF)
        parts.append((high, (stack - high.astype(F32)).astype(BF)))
    left = jnp.concatenate([parts[0][0], parts[1][0], parts[0][1], parts[1][1]], axis=1)
    src = iota((512, 256), 0)
    dst = iota((512, 256), 1)
    half_src = lax.rem(src, 128)
    want = (half_src // 64) * 128 + 2 * lax.rem(half_src, 64) + lax.rem(src // 128, 2)
    res = dot(left, (dst == want).astype(BF))
    for k in range(2):
        spill[k] = res[:, 128 * k : 128 * k + 128]
    for c in range(2):
        for dr in range(2):
            for k in range(2):
                tend[c, pl.ds(2 * k + dr, pairs4 // 2, stride=4), :] = spill[
                    k, pl.ds(dr * 2 + c, pairs4 // 2, stride=8), :
                ]
    land = land_ref[...].astype(F32)
    for c in range(2):
        total = vel_ref[c].astype(F32) + (tend[c] + b4_ref[c])
        out_ref[c] = (land * total).astype(BF)


def pack_first(w):
    flat = w.reshape(5, 10, w.shape[3])
    lead = 3 * SLOT
    return jnp.stack(
        [
            jnp.pad(
                jnp.pad(flat, ((0, 0), (2 * b, SLOT - 10 - 2 * b), (0, 0))).reshape(5 * SLOT, -1),
                ((lead, lead), (0, 0)),
            )
            for b in range(6)
        ]
    )


def pack_second(w):
    ends = [jnp.pad(w, ((0, 0), (k, 1 - k), (0, 0), (0, 0))) for k in range(2)]
    both = jnp.concatenate(ends, axis=3)
    return both.reshape(5, 6 * w.shape[2], 2 * w.shape[3])


def blocks(w):
    parts = [
        jnp.pad(w, ((dr, 1 - dr), (dc, 1 - dc), (0, 0), (0, 0))) for dr in range(2) for dc in range(2)
    ]
    both = jnp.stack(parts, axis=3).reshape(2, 2, 2, 2, w.shape[2], 2, 2, w.shape[3])
    return both.transpose(0, 2, 1, 3, 4, 5, 6, 7)


def pack_third(w):
    return blocks(w).reshape(16 * w.shape[2], 4 * w.shape[3])


def pack_fourth(w):
    both = blocks(w).reshape(16 * w.shape[2], 2, 2, w.shape[3])
    both = both.transpose(2, 1, 3, 0).reshape(2, 2 * w.shape[3], -1)
    return jnp.pad(both, ((0, 0), (0, 8 - both.shape[1]), (0, 0))).reshape(16, -1)


def shards(velocity, land_sea, fold_pivot, w1, b1, w2, b2, w3, b3, w4, b4):
    rows = velocity.shape[2]
    cols = velocity.shape[3]
    n = lax.axis_size("lon")
    vel = velocity.reshape(2, rows, cols)
    land = land_sea.reshape(rows, cols)
    own = vel * land.astype(BF)[None]
    mirror = [(i, n - 1 - i) for i in range(n)]
    pairs_a = [(i, i ^ 1) for i in range(n)]
    pairs_b = [(0, 0), (n - 1, n - 1)]
    for k in range(1, n // 2):
        pairs_b += [(2 * k - 1, 2 * k), (2 * k, 2 * k - 1)]
    far = lax.ppermute(own, "lon", mirror)
    both = jnp.concatenate([own, far[:, rows - 8 :]], axis=1)
    near_a = lax.ppermute(both, "lon", pairs_a)
    near_b = lax.ppermute(both, "lon", pairs_b)
    vmem = pl.BlockSpec(memory_space=pltpu.VMEM)
    smem = pl.BlockSpec(memory_space=pltpu.SMEM)
    ext = rows + 12
    groups = (rows + 8) // 4
    pairs = (rows + 4) // 2
    return pl.pallas_call(
        functools.partial(body, lon_count=n),
        out_shape=jax.ShapeDtypeStruct((2, rows, cols), BF),
        in_specs=[smem, smem] + [vmem] * 13,
        out_specs=vmem,
        scratch_shapes=[
            pltpu.VMEM((1, ext * SLOT, cols), F32),
            pltpu.VMEM((2, ext * SLOT, cols), F32),
            pltpu.VMEM((64, ext * SLOT), BF),
            pltpu.VMEM((64, ext * SLOT), BF),
            pltpu.VMEM((EDGE, ext * SLOT), F32),
            pltpu.VMEM((2, 3, 2 * groups, 64, 256), BF),
            pltpu.VMEM((2, 3, 6, 64, 256), BF),
            pltpu.VMEM((2, 3, 2 * groups * EDGE, 256), F32),
            pltpu.VMEM((pairs * 72 + 8, 256), F32),
            pltpu.VMEM((pairs * 72 + 8, 128), F32),
            pltpu.VMEM((8, 2 * cols), F32),
            pltpu.VMEM((2, 64, 128), F32),
            pltpu.VMEM((2, rows, cols), F32),
        ],
        compiler_params=pltpu.CompilerParams(vmem_limit_bytes=40 << 20),
    )(
        fold_pivot,
        b4,
        vel,
        land,
        own,
        far,
        near_a,
        near_b,
        pack_first(w1),
        b1[None],
        pack_second(w2),
        b2[None],
        pack_third(w3),
        b3[None],
        pack_fourth(w4),
    ).reshape(velocity.shape)


def solution(mesh):
    in_specs = (
        P(None, ("members", "lev"), None, "lon"),
        P(("members", "lev"), None, "lon"),
    ) + (P(),) * 9
    out_specs = P(None, ("members", "lev"), None, "lon")
    return jax.shard_map(shards, mesh=mesh, in_specs=in_specs, out_specs=out_specs, check_vma=False)
```

```python
import functools

import jax
import jax.numpy as jnp
from jax import lax
from jax.experimental import pallas as pl
from jax.experimental.pallas import tpu as pltpu
from jax.sharding import PartitionSpec as P

BF = jnp.bfloat16
F32 = jnp.float32
EDGE = 8
LINE = 72
SPLIT = 8


def dot(a, b):
    return jnp.dot(a, b, preferred_element_type=F32)


def dot_nt(a, b):
    return lax.dot_general(a, b, (((1,), (1,)), ((), ())), preferred_element_type=F32)


def iota(shape, dim):
    return lax.broadcasted_iota(jnp.int32, shape, dim)


def roll_lanes(x, shift):
    return pltpu.roll(x, shift % x.shape[1], axis=1)


def first_weights(w1_ref, row, half):
    zero = jnp.zeros(w1_ref.shape[2:], BF)
    sides = []
    for b in (2 * half, 2 * half + 1):
        tiles = [w1_ref[row, t - b] if 0 <= t - b < 5 else zero for t in range(10)]
        sides.append(jnp.concatenate(tiles, axis=0))
    return jnp.concatenate(sides, axis=1)


def load_field(field_ref, values):
    rows = values[0].shape[0]
    for c in range(2):
        field_ref[c, 0:8, :] = jnp.zeros((8, values[0].shape[1]), F32)
        field_ref[c, rows : rows + 16, :] = jnp.zeros((16, values[0].shape[1]), F32)
        field_ref[c, 6 : rows + 6, :] = values[c]


def load_fold(fold_ref, tails):
    for c in range(2):
        fold_ref[c] = jnp.zeros(fold_ref.shape[1:], F32)
        for k in range(1, 7):
            fold_ref[c, 5 + k : 6 + k, :] = -tails[c][7 - k : 8 - k]


def patches(ref, start, shifted):
    tiles = []
    windows = [ref[c, start : start + 8, :] for c in range(2)]
    for t in range(10):
        tiles.append(jnp.concatenate([shifted(windows[c], t, c) for c in range(2)], axis=0))
    return jnp.concatenate(tiles, axis=0).astype(BF)


def left_sides(field_ref, fold_ref, pivot_ref, wide, pick, pick_fold, groups, rows):
    out = []
    for g in groups:
        part = dot_nt(pick, patches(field_ref, 4 * g, lambda x, t, c: roll_lanes(x, -t)))
        if 4 * g + 8 > rows + 6:
            ups = [pivot_ref[c] - (wide - 1) > 0 for c in range(2)]

            def turned(x, t, c):
                return jnp.where(ups[c], roll_lanes(x, t - 1), roll_lanes(x, t + 1))

            part = part + dot_nt(pick_fold, patches(fold_ref, 4 * g - rows, turned))
        out.append(part)
    return out


def second_weights(w2_ref):
    zero = jnp.zeros(w2_ref.shape[2:], BF)
    rows = []
    for dr in range(2):
        for dc in range(2):
            rows.append(
                jnp.concatenate(
                    [
                        w2_ref[a - dr, b - dc] if 0 <= a - dr < 5 and 0 <= b - dc < 5 else zero
                        for a in range(6)
                        for b in range(6)
                    ],
                    axis=1,
                )
            )
    return jnp.concatenate(rows, axis=0)


def block_weights(w_ref):
    zero = jnp.zeros(w_ref.shape[2:], F32)
    rows = []
    for dr in range(2):
        for dc in range(2):
            cells = []
            for er in range(2):
                for ec in range(2):
                    for r in range(2):
                        for c in range(2):
                            a, b = 2 * er + r - dr, 2 * ec + c - dc
                            inside = 0 <= a < 3 and 0 <= b < 3
                            cells.append(w_ref[a, b].astype(F32) if inside else zero)
            rows.append(jnp.concatenate(cells, axis=1))
    return rows


def mask_body(vel_hbm, land_hbm, own_ref, vel_ref, land_ref, sems):
    copies = [
        pltpu.make_async_copy(vel_hbm, vel_ref, sems.at[0]),
        pltpu.make_async_copy(land_hbm, land_ref, sems.at[1]),
    ]
    for copy in copies:
        copy.start()
    for copy in copies:
        copy.wait()
    land = land_ref[...].astype(F32)
    for c in range(2):
        own_ref[c] = (vel_ref[c].astype(F32) * land).astype(BF)


def pack_first(w1_ref, wide_ref, w1_out):
    wide_ref[...] = jnp.zeros_like(wide_ref)
    for t in range(5):
        for a in range(5):
            value = w1_ref[a, t].astype(F32)
            for row in range(4):
                for c in range(2):
                    at = 8 * c + row + a
                    wide_ref[row, t, at : at + 1, :] = value[c : c + 1]
    w1_out[...] = wide_ref[...].astype(BF)


def first_layer(stacked, w1_ref, bias, put):
    for row in range(4):
        for half in range(3):
            res = dot(stacked, first_weights(w1_ref, row, half))
            put(row, half, jnp.maximum(res + bias, 0.0))


def second_layer(f_ref, right, bias, sec_ref, start, count, step):
    for lo in range(0, count, step):
        left = jnp.concatenate(
            [
                f_ref[a % 2, half, lo + a // 2 : lo + a // 2 + step].reshape(step * 64, 256)
                for a in range(6)
                for half in range(3)
            ],
            axis=1,
        )
        res = jnp.maximum(dot_nt(left, right) + bias, 0.0)
        for k in range(step):
            at = (start + lo + k) * LINE
            sec_ref[at : at + 64, :] = res[64 * k : 64 * k + 64]


def inner_first(lefts, f_ref, flat_ref, w1_ref, bias):
    stacked = jnp.concatenate(lefts, axis=0).astype(BF)
    size = stacked.shape[0]
    for row in range(4):
        res = dot(stacked, first_weights(w1_ref, row, 0))
        flat_ref[row, 0:size, :] = jnp.maximum(res + bias, 0.0)
        for half in range(3):
            for g in range(len(lefts)):
                at = 64 * g + half
                f_ref[row % 2, half, 2 * g + row // 2] = flat_ref[row, at : at + 64, :].astype(BF)


def inner_picks(cols):
    lane = iota((64, cols), 1)
    slot = iota((64, cols), 0)
    fold = lax.rem(2 * cols + 5 - 2 * slot, cols)
    return (lane == 2 * slot - 6).astype(BF), (lane == fold).astype(BF)


def south_body(
    own_ref, w1_hbm, b1_hbm, w2_hbm, b2_hbm, sec, w1_out, field, f, flat, wide, w1_ref, b1_ref,
    w2_ref, b2_ref, sems,
):
    moves = [(w1_hbm, w1_ref), (b1_hbm, b1_ref), (w2_hbm, w2_ref), (b2_hbm, b2_ref)]
    copies = [pltpu.make_async_copy(a, b, sems.at[k]) for k, (a, b) in enumerate(moves)]
    for copy in copies:
        copy.start()
    rows = own_ref.shape[1]
    cols = own_ref.shape[2]
    load_field(field, [own_ref[c].astype(F32) for c in range(2)])
    pick, _ = inner_picks(cols)
    lefts = left_sides(field, None, None, 0, pick, None, range(SPLIT // 2 + 1), rows)
    copies[0].wait()
    pack_first(w1_ref, wide, w1_out)
    copies[1].wait()
    inner_first(lefts, f, flat, w1_out, jnp.concatenate([b1_ref[...]] * 2, axis=1))
    copies[2].wait()
    copies[3].wait()
    bias2 = jnp.concatenate([b2_ref[...]] * 4, axis=1)
    second_layer(f, second_weights(w2_ref), bias2, sec, 0, SPLIT, SPLIT // 2)


def north_body(
    pivot_ref, own_ref, far_ref, w1_ref, b1_ref, w2_ref, b2_ref, w3_ref, w4_ref, sec_in,
    sec, w3_out, w4_out, sel_out, field, fold, f, flat, *, lon_count, step,
):
    bias1 = jnp.concatenate([b1_ref[...]] * 2, axis=1)
    bias2 = jnp.concatenate([b2_ref[...]] * 4, axis=1)
    rows = own_ref.shape[1]
    cols = own_ref.shape[2]
    w3_out[...] = jnp.concatenate(block_weights(w3_ref), axis=0).astype(BF)
    tiny = block_weights(w4_ref)
    blank = jnp.zeros((4, tiny[0].shape[1]), F32)
    order = [tiny[0], tiny[2], blank, tiny[1], tiny[3], blank]
    w4_out[...] = jnp.concatenate(order, axis=0).astype(BF)
    src = iota((256, 256), 0)
    want = 2 * (src & 127) + (src >> 7)
    sel_out[...] = (iota((256, 256), 1) == want).astype(BF)
    load_field(field, [own_ref[c].astype(F32) for c in range(2)])
    load_fold(fold, [far_ref[c, rows - 8 :].astype(F32) for c in range(2)])
    pick, pick_fold = inner_picks(cols)
    groups = range(SPLIT // 2, (rows + 8) // 4)
    lefts = left_sides(field, fold, pivot_ref, lon_count * cols, pick, pick_fold, groups, rows)
    inner_first(lefts, f, flat, w1_ref, bias1)
    count = (rows + 4) // 2 - SPLIT
    second_layer(f, second_weights(w2_ref), bias2, sec, SPLIT, count, step)


def last_body(
    pivot_ref, b4_ref, vel_ref, land_ref, own_ref, far_ref, near_a_ref, near_b_ref,
    w1_ref, b1_ref, w2_ref, b2_ref, w3_ref, b3_ref, w4_ref, sel_ref, sec_in,
    out_ref, sec, field, fold, f, third, spill, tend, *, lon_count,
):
    rows = own_ref.shape[1]
    cols = own_ref.shape[2]
    bias1 = jnp.concatenate([b1_ref[...]] * 2, axis=1)
    bias2 = jnp.concatenate([b2_ref[...]] * 4, axis=1)
    bias3 = jnp.concatenate([b3_ref[...]] * 4, axis=1)
    groups = (rows + 8) // 4
    pairs = (rows + 4) // 2

    lon = lax.axis_index("lon")
    even = lax.rem(lon, 2) == 0
    own = own_ref[...].astype(F32)
    far = far_ref[...].astype(F32)
    wrap = jnp.concatenate([far, own[:, rows - 8 :]], axis=1)
    near_a = near_a_ref[...].astype(F32)
    near_b = near_b_ref[...].astype(F32)
    west = jnp.where(lon == 0, wrap, jnp.where(even, near_b, near_a))
    east = jnp.where(lon == lon_count - 1, wrap, jnp.where(even, near_a, near_b))

    def around(mid, after, before):
        lane = iota(mid.shape, 1)
        half, quarter = cols // 2, cols // 4
        moved = jnp.where(lane < quarter, after, roll_lanes(mid, half))
        moved = jnp.where((lane >= quarter) & (lane < half), roll_lanes(before, half), moved)
        return jnp.where(lane >= half + quarter, mid, moved)

    load_field(field, [around(own[c], east[c, :rows], west[c, :rows]) for c in range(2)])
    load_fold(fold, [around(far[c, rows - 8 :], west[c, rows:], east[c, rows:]) for c in range(2)])
    slot = lax.rem(iota((16, cols), 0), EDGE)
    lane = iota((16, cols), 1)
    high = jnp.where(slot < 6, 60, 56)
    pair = jnp.where(slot < 4, slot, slot + high)
    start = jnp.where(slot < 4, 2 * pair - 6 + cols // 2, 2 * pair - 6)
    pick = (lane == lax.rem(start + cols, cols)).astype(BF)
    start = jnp.where(slot < 4, cols + 5 - 2 * pair, cols + 5 - 2 * pair + cols // 2)
    pick_fold = (lane == lax.rem(start + cols, cols)).astype(BF)
    lefts = left_sides(
        field, fold, pivot_ref, lon_count * cols, pick, pick_fold, range(groups), rows
    )
    stacked = jnp.concatenate([x[:EDGE] for x in lefts], axis=0).astype(BF)

    def put(row, half, res):
        for g in range(groups):
            at = (2 * g + row // 2) * EDGE
            f[row % 2, half, at : at + EDGE, :] = res[EDGE * g : EDGE * g + EDGE]

    first_layer(stacked, w1_ref, bias1, put)
    right = second_weights(w2_ref)
    sums = []
    for low in (0, 3):
        left = jnp.concatenate(
            [
                f[a % 2, half, (a // 2) * EDGE : (a // 2 + pairs) * EDGE, :].astype(BF)
                for a in range(low, low + 3)
                for half in range(3)
            ],
            axis=1,
        )
        sums.append(dot_nt(left, right[:, low * 768 : low * 768 + 2304]))
    res = jnp.maximum(sums[0] + sums[1] + bias2, 0.0)
    line = iota((EDGE, 256), 0)
    for k in range(pairs):
        new = res[EDGE * k : EDGE * k + EDGE]
        at = k * LINE
        sec[at : at + 8, :] = jnp.where(line < 4, new, sec_in[at : at + 8, :])
        sec[at + 56 : at + 64, :] = jnp.where(line >= 6, new, sec_in[at + 56 : at + 64, :])
        sec[at + 64 : at + 72, :] = pltpu.roll(new, 4, axis=0)

    pairs3 = pairs - 1
    right = w3_ref[...]
    middle = (pairs3 + 1) // 2
    for lo, hi in ((0, middle), (middle, pairs3)):
        base, size = lo * LINE, (hi - lo) * LINE
        left = jnp.concatenate(
            [
                sec[base + at : base + at + size, :].astype(BF)
                for at in (0, 1, LINE, LINE + 1)
            ],
            axis=1,
        )
        third[base : base + size, :] = jnp.maximum(dot_nt(left, right) + bias3, 0.0)

    pairs4 = pairs - 2
    right = w4_ref[...]
    tiles = []
    for lo in (0, pairs4 // 2):
        left = jnp.concatenate(
            [
                jnp.concatenate(
                    [
                        third[k * LINE + at : k * LINE + at + 64, :]
                        for k in range(lo, lo + pairs4 // 2)
                    ],
                    axis=0,
                ).astype(BF)
                for at in (0, 1, LINE, LINE + 1)
            ],
            axis=1,
        )
        res = dot_nt(right, left)
        tiles += [res[:, 128 * t : 128 * t + 128] for t in range(pairs4 // 4)]
    stack = jnp.concatenate(
        [jnp.concatenate([x[8 * dc : 8 * dc + 8] for x in tiles], axis=0) for dc in range(2)], axis=1
    )
    upper = stack.astype(BF)
    lower = (stack - upper.astype(F32)).astype(BF)
    res = dot(jnp.concatenate([upper, lower], axis=0), sel_ref[...])
    count = 8 * len(tiles)
    res = res[:count] + res[count:]
    for k in range(2):
        spill[k] = res[:, 128 * k : 128 * k + 128]
    for c in range(2):
        for dr in range(2):
            for k in range(2):
                tend[c, pl.ds(2 * k + dr, pairs4 // 2, stride=4), :] = spill[
                    k, pl.ds(dr * 2 + c, pairs4 // 2, stride=8), :
                ]
    land = land_ref[...].astype(F32)
    for c in range(2):
        total = vel_ref[c].astype(F32) + (tend[c] + b4_ref[c])
        out_ref[c] = (land * total).astype(BF)


def call(fn, ins, outs, scratch, scalars=0, flops=0, aliases=None, far_ins=()):
    vmem = pl.BlockSpec(memory_space=pltpu.VMEM)
    smem = pl.BlockSpec(memory_space=pltpu.SMEM)
    hbm = pl.BlockSpec(memory_space=pltpu.HBM)
    specs = [smem] * scalars + [vmem] * (len(ins) - scalars)
    ins = list(ins)
    for k in far_ins:
        specs[k] = hbm
        ins[k] = pltpu.with_memory_space_constraint(ins[k], pltpu.HBM)
    return pl.pallas_call(
        fn,
        out_shape=outs,
        in_specs=specs,
        out_specs=[vmem] * len(outs),
        scratch_shapes=scratch,
        input_output_aliases=aliases or {},
        cost_estimate=pl.CostEstimate(flops=flops, bytes_accessed=1 << 20, transcendentals=0),
        compiler_params=pltpu.CompilerParams(
            vmem_limit_bytes=32 << 20
        ),
    )(*ins)


def step(velocity, land_sea, fold_pivot, w1, b1, w2, b2, w3, b3, w4, b4):
    rows = velocity.shape[2]
    cols = velocity.shape[3]
    n = lax.axis_size("lon")
    vel = velocity.reshape(2, rows, cols)
    land = land_sea.reshape(rows, cols)
    w2, w3, w4 = (jnp.swapaxes(w, 2, 3) for w in (w2, w3, w4))
    b1, b2, b3 = b1[None], b2[None], b3[None]
    shape = jax.ShapeDtypeStruct
    scratch = pltpu.VMEM
    sems = pltpu.SemaphoreType.DMA
    (own,) = call(
        mask_body,
        [vel, land],
        [shape(vel.shape, BF)],
        [scratch(vel.shape, BF), scratch(land.shape, jnp.int32), sems((2,))],
        far_ins=(0, 1),
    )
    mirror = [(i, n - 1 - i) for i in range(n)]
    pairs_a = [(i, i ^ 1) for i in range(n)]
    pairs_b = [(0, 0), (n - 1, n - 1)]
    for k in range(1, n // 2):
        pairs_b += [(2 * k - 1, 2 * k), (2 * k, 2 * k - 1)]
    far = lax.ppermute(own, "lon", mirror)
    groups = (rows + 8) // 4
    pairs = (rows + 4) // 2
    sec_shape = shape((pairs * LINE + 8, 256), F32)
    south_groups = SPLIT // 2 + 1
    north_groups = groups - SPLIT // 2
    packed = (4, 5, 16, w1.shape[3])
    field = scratch((2, rows + 16, cols), F32)
    fold = scratch((2, 16, cols), F32)
    sec, w1_wide = call(
        south_body,
        [own, w1, b1, w2, b2],
        [sec_shape, shape(packed, BF)],
        [field, scratch((2, 3, 2 * south_groups, 64, 256), BF)]
        + [scratch((4, 64 * south_groups + 8, 256), F32), scratch(packed, F32)]
        + [scratch(x.shape, x.dtype) for x in (w1, b1, w2, b2)]
        + [sems((4,))],
        flops=2 * 64 * SPLIT * 256 * 4608,
        far_ins=(1, 2, 3, 4),
    )
    both = jnp.concatenate([own, far[:, rows - 8 :]], axis=1)
    near_a = lax.ppermute(both, "lon", pairs_a)
    near_b = lax.ppermute(both, "lon", pairs_b)
    sec, w3_wide, w4_wide, sel = call(
        functools.partial(north_body, lon_count=n, step=(pairs - SPLIT) // 2),
        [fold_pivot, own, far, w1_wide, b1, w2, b2, w3, w4, sec],
        [sec_shape, shape((128, 1024), BF), shape((16, 512), BF), shape((256, 256), BF)],
        [field, fold, scratch((2, 3, 2 * north_groups, 64, 256), BF)]
        + [scratch((4, 64 * north_groups + 8, 256), F32)],
        scalars=1,
        flops=2 * 64 * (pairs - SPLIT) * 256 * 4608,
        aliases={9: 0},
    )
    out, _ = call(
        functools.partial(last_body, lon_count=n),
        [fold_pivot, b4, vel, land, own, far, near_a, near_b]
        + [w1_wide, b1, w2, b2, w3_wide, b3, w4_wide, sel, sec],
        [shape((2, rows, cols), BF), sec_shape],
        [
            field,
            fold,
            scratch((2, 3, 2 * groups * EDGE, 256), F32),
            scratch((pairs * LINE + 8, 128), F32),
            scratch((2, 64, 128), F32),
            scratch((2, rows, cols), F32),
        ],
        scalars=2,
        flops=2 * 64 * pairs * 256 * 1024,
        aliases={16: 1},
    )
    return out.reshape(velocity.shape)


def solution(mesh):
    in_specs = (
        P(None, ("members", "lev"), None, "lon"),
        P(("members", "lev"), None, "lon"),
    ) + (P(),) * 9
    out_specs = P(None, ("members", "lev"), None, "lon")
    return jax.shard_map(step, mesh=mesh, in_specs=in_specs, out_specs=out_specs, check_vma=False)
```

```python
import functools

import jax
import jax.numpy as jnp
from jax import lax
from jax.experimental import pallas as pl
from jax.experimental.pallas import tpu as pltpu
from jax.sharding import PartitionSpec as P

BF = jnp.bfloat16
F32 = jnp.float32
EDGE = 8
LINE = 72
SPLIT = 8


def dot(a, b):
    return jnp.dot(a, b, preferred_element_type=F32)


def dot_nt(a, b):
    return lax.dot_general(a, b, (((1,), (1,)), ((), ())), preferred_element_type=F32)


def iota(shape, dim):
    return lax.broadcasted_iota(jnp.int32, shape, dim)


def roll_lanes(x, shift):
    return pltpu.roll(x, shift % x.shape[1], axis=1)


def first_weights(w1_ref, row):
    zero = jnp.zeros(w1_ref.shape[2:], BF)
    sides = []
    for b in range(2):
        tiles = [w1_ref[row, t - b] if 0 <= t - b < 5 else zero for t in range(6)]
        sides.append(jnp.concatenate(tiles, axis=0))
    return jnp.concatenate(sides, axis=1)


def load_field(field_ref, values):
    rows = values[0].shape[0]
    for c in range(2):
        field_ref[c, 0:8, :] = jnp.zeros((8, values[0].shape[1]), F32)
        field_ref[c, rows : rows + 16, :] = jnp.zeros((16, values[0].shape[1]), F32)
        field_ref[c, 6 : rows + 6, :] = values[c]


def load_fold(fold_ref, tails):
    for c in range(2):
        fold_ref[c] = jnp.zeros(fold_ref.shape[1:], F32)
        for k in range(1, 7):
            fold_ref[c, 5 + k : 6 + k, :] = -tails[c][7 - k : 8 - k]


def patches(ref, start, shifted):
    tiles = []
    windows = [ref[c, start : start + 8, :] for c in range(2)]
    for t in range(6):
        tiles.append(jnp.concatenate([shifted(windows[c], t, c) for c in range(2)], axis=0))
    return jnp.concatenate(tiles, axis=0).astype(BF)


def left_sides(field_ref, fold_ref, pivot_ref, wide, pick, pick_fold, groups, rows):
    out = []
    for g in groups:
        part = dot_nt(pick, patches(field_ref, 4 * g, lambda x, t, c: roll_lanes(x, -t)))
        if 4 * g + 8 > rows + 6:
            ups = [pivot_ref[c] - (wide - 1) > 0 for c in range(2)]

            def turned(x, t, c):
                return jnp.where(ups[c], roll_lanes(x, t - 1), roll_lanes(x, t + 1))

            part = part + dot_nt(pick_fold, patches(fold_ref, 4 * g - rows, turned))
        out.append(part)
    return out


def second_weights(w2_ref):
    zero = jnp.zeros(w2_ref.shape[2:], BF)
    rows = []
    for shift in range(3):
        for dr in range(2):
            for dc in range(2):
                cells = []
                for a in range(6):
                    for b in (2 * shift - dc, 2 * shift + 1 - dc):
                        inside = 0 <= a - dr < 5 and 0 <= b < 5
                        cells.append(w2_ref[a - dr, b] if inside else zero)
                rows.append(jnp.concatenate(cells, axis=1))
    return jnp.concatenate(rows, axis=0)


def block_weights(w_ref, shifts):
    zero = jnp.zeros(w_ref.shape[2:], F32)
    rows = []
    for dr in range(2):
        for dc in range(2):
            cells = []
            for er in range(2):
                for ec in shifts:
                    for r in range(2):
                        for c in range(2):
                            a, b = 2 * er + r - dr, 2 * ec + c - dc
                            inside = 0 <= a < 3 and 0 <= b < 3
                            cells.append(w_ref[a, b].astype(F32) if inside else zero)
            rows.append(jnp.concatenate(cells, axis=1))
    return rows


def mask_body(vel_hbm, land_hbm, own_ref, vel_ref, land_ref, sems):
    copies = [
        pltpu.make_async_copy(vel_hbm, vel_ref, sems.at[0]),
        pltpu.make_async_copy(land_hbm, land_ref, sems.at[1]),
    ]
    for copy in copies:
        copy.start()
    for copy in copies:
        copy.wait()
    land = land_ref[...].astype(F32)
    for c in range(2):
        own_ref[c] = (vel_ref[c].astype(F32) * land).astype(BF)


def pack_first(w1_ref, wide_ref, w1_out):
    wide_ref[...] = jnp.zeros_like(wide_ref)
    for t in range(5):
        for a in range(5):
            value = w1_ref[a, t].astype(F32)
            for row in range(4):
                for c in range(2):
                    at = 8 * c + row + a
                    wide_ref[row, t, at : at + 1, :] = value[c : c + 1]
    w1_out[...] = wide_ref[...].astype(BF)


def first_layer(lefts, f_ref, w1_ref, bias):
    stacked = jnp.concatenate(lefts, axis=0).astype(BF)
    size = lefts[0].shape[0]
    for row in range(4):
        res = dot(stacked, first_weights(w1_ref, row))
        res = jnp.maximum(res + bias, 0.0).astype(BF)
        for g in range(len(lefts)):
            f_ref[row % 2, 2 * g + row // 2] = res[size * g : size * g + size]


def second_layer(f_ref, right, acc_ref, lo, count):
    size = f_ref.shape[2]
    left = jnp.concatenate(
        [
            f_ref[a % 2, lo + a // 2 : lo + a // 2 + count].reshape(count * size, 256)
            for a in range(6)
        ],
        axis=1,
    )
    res = dot_nt(left, right)
    for shift in range(3):
        acc_ref[shift, 0 : count * size, :] = res[:, 256 * shift : 256 * shift + 256]


def shifted_sum(acc_ref, at, size, bias):
    parts = [acc_ref[k, at + k : at + k + size, :] for k in range(acc_ref.shape[0])]
    total = parts[0]
    for part in parts[1:]:
        total = total + part
    return jnp.maximum(total + bias, 0.0)


def inner_second(f_ref, right, bias, acc_ref, sec_ref, start, count):
    chunks = acc_ref.shape[0]
    step = count // chunks
    for k in range(chunks):
        second_layer(f_ref, right, acc_ref.at[k], k * step, step)
        for p in range(step):
            at = (start + k * step + p) * LINE
            sec_ref[at : at + 64, :] = shifted_sum(acc_ref.at[k], 64 * p, 64, bias)


def inner_picks(cols):
    lane = iota((64, cols), 1)
    slot = iota((64, cols), 0)
    fold = lax.rem(2 * cols + 5 - 2 * slot, cols)
    return (lane == 2 * slot - 6).astype(BF), (lane == fold).astype(BF)


def south_body(
    own_ref, w1_hbm, b1_hbm, w2_hbm, b2_hbm, sec, w1_out, field, f, acc, wide, w1_ref, b1_ref,
    w2_ref, b2_ref, sems,
):
    moves = [(w1_hbm, w1_ref), (b1_hbm, b1_ref), (w2_hbm, w2_ref), (b2_hbm, b2_ref)]
    copies = [pltpu.make_async_copy(a, b, sems.at[k]) for k, (a, b) in enumerate(moves)]
    for copy in copies:
        copy.start()
    rows = own_ref.shape[1]
    cols = own_ref.shape[2]
    load_field(field, [own_ref[c].astype(F32) for c in range(2)])
    pick, _ = inner_picks(cols)
    lefts = left_sides(field, None, None, 0, pick, None, range(SPLIT // 2 + 1), rows)
    copies[0].wait()
    pack_first(w1_ref, wide, w1_out)
    copies[1].wait()
    first_layer(lefts, f, w1_out, jnp.concatenate([b1_ref[...]] * 2, axis=1))
    copies[2].wait()
    copies[3].wait()
    bias2 = jnp.concatenate([b2_ref[...]] * 4, axis=1)
    inner_second(f, second_weights(w2_ref), bias2, acc, sec, 0, SPLIT)


def north_body(
    pivot_ref, own_ref, far_ref, w1_ref, b1_ref, w2_ref, b2_ref, w3_ref, w4_ref, sec_in,
    sec, w3_out, w4_out, sel_out, field, fold, f, acc, *, lon_count,
):
    bias1 = jnp.concatenate([b1_ref[...]] * 2, axis=1)
    bias2 = jnp.concatenate([b2_ref[...]] * 4, axis=1)
    rows = own_ref.shape[1]
    cols = own_ref.shape[2]
    blocks = block_weights(w3_ref, (0,)) + block_weights(w3_ref, (1,))
    w3_out[...] = jnp.concatenate(blocks, axis=0).astype(BF)
    tiny = block_weights(w4_ref, (0, 1))
    blank = jnp.zeros((4, tiny[0].shape[1]), F32)
    order = [tiny[0], tiny[2], blank, tiny[1], tiny[3], blank]
    w4_out[...] = jnp.concatenate(order, axis=0).astype(BF)
    src = iota((256, 256), 0)
    want = 2 * (src & 127) + (src >> 7)
    sel_out[...] = (iota((256, 256), 1) == want).astype(BF)
    load_field(field, [own_ref[c].astype(F32) for c in range(2)])
    load_fold(fold, [far_ref[c, rows - 8 :].astype(F32) for c in range(2)])
    pick, pick_fold = inner_picks(cols)
    groups = range(SPLIT // 2, (rows + 8) // 4)
    lefts = left_sides(field, fold, pivot_ref, lon_count * cols, pick, pick_fold, groups, rows)
    first_layer(lefts, f, w1_ref, bias1)
    count = (rows + 4) // 2 - SPLIT
    inner_second(f, second_weights(w2_ref), bias2, acc, sec, SPLIT, count)


def last_body(
    pivot_ref, b4_ref, vel_ref, land_ref, own_ref, far_ref, near_a_ref, near_b_ref,
    w1_ref, b1_ref, w2_ref, b2_ref, w3_ref, b3_ref, w4_ref, sel_ref, sec_in,
    out_ref, sec, field, fold, f, acc, acc3, third, spill, tend, *, lon_count,
):
    rows = own_ref.shape[1]
    cols = own_ref.shape[2]
    bias1 = jnp.concatenate([b1_ref[...]] * 2, axis=1)
    bias2 = jnp.concatenate([b2_ref[...]] * 4, axis=1)
    bias3 = jnp.concatenate([b3_ref[...]] * 4, axis=1)
    groups = (rows + 8) // 4
    pairs = (rows + 4) // 2

    lon = lax.axis_index("lon")
    even = lax.rem(lon, 2) == 0
    own = own_ref[...].astype(F32)
    far = far_ref[...].astype(F32)
    wrap = jnp.concatenate([far, own[:, rows - 8 :]], axis=1)
    near_a = near_a_ref[...].astype(F32)
    near_b = near_b_ref[...].astype(F32)
    west = jnp.where(lon == 0, wrap, jnp.where(even, near_b, near_a))
    east = jnp.where(lon == lon_count - 1, wrap, jnp.where(even, near_a, near_b))

    def around(mid, after, before):
        lane = iota(mid.shape, 1)
        half, quarter = cols // 2, cols // 4
        moved = jnp.where(lane < quarter, after, roll_lanes(mid, half))
        moved = jnp.where((lane >= quarter) & (lane < half), roll_lanes(before, half), moved)
        return jnp.where(lane >= half + quarter, mid, moved)

    load_field(field, [around(own[c], east[c, :rows], west[c, :rows]) for c in range(2)])
    load_fold(fold, [around(far[c, rows - 8 :], west[c, rows:], east[c, rows:]) for c in range(2)])
    slot = iota((2 * EDGE, cols), 0)
    lane = iota((2 * EDGE, cols), 1)
    low = slot < EDGE
    pair = jnp.where(low, slot, slot + (cols // 2 - 2 - EDGE))
    start = 2 * pair - 6 + jnp.where(low, cols // 2, 0)
    pick = (lane == lax.rem(start + cols, cols)).astype(BF)
    start = cols + 5 - 2 * pair + jnp.where(low, 0, cols // 2)
    pick_fold = (lane == lax.rem(start + cols, cols)).astype(BF)
    lefts = left_sides(
        field, fold, pivot_ref, lon_count * cols, pick, pick_fold, range(groups), rows
    )
    first_layer(lefts, f, w1_ref, bias1)
    second_layer(f, second_weights(w2_ref), acc, 0, pairs)
    line = iota((EDGE, 256), 0)
    for k in range(pairs):
        at = k * LINE
        new = shifted_sum(acc, 2 * EDGE * k, EDGE, bias2)
        sec[at : at + 8, :] = jnp.where(line < 4, new, sec_in[at : at + 8, :])
        new = pltpu.roll(shifted_sum(acc, 2 * EDGE * k + EDGE, EDGE, bias2), 6, axis=0)
        sec[at + 56 : at + 64, :] = jnp.where(line >= 6, new, sec_in[at + 56 : at + 64, :])
        sec[at + 64 : at + 72, :] = new

    pairs3 = pairs - 1
    right = w3_ref[...]
    middle = (pairs3 + 1) // 2
    for part, (lo, hi) in enumerate(((0, middle), (middle, pairs3))):
        base, size = lo * LINE, (hi - lo) * LINE
        left = [sec[base + at : base + at + size, :].astype(BF) for at in (0, LINE)]
        res = dot_nt(jnp.concatenate(left, axis=1), right)
        for shift in range(2):
            acc3[part, shift, 0:size, :] = res[:, 128 * shift : 128 * shift + 128]
        third[base : base + size, :] = shifted_sum(acc3.at[part], 0, size, bias3)

    pairs4 = pairs - 2
    right = w4_ref[...]
    tiles = []
    for lo in (0, pairs4 // 2):
        left = jnp.concatenate(
            [
                jnp.concatenate(
                    [
                        third[k * LINE + at : k * LINE + at + 64, :]
                        for k in range(lo, lo + pairs4 // 2)
                    ],
                    axis=0,
                ).astype(BF)
                for at in (0, 1, LINE, LINE + 1)
            ],
            axis=1,
        )
        res = dot_nt(right, left)
        tiles += [res[:, 128 * t : 128 * t + 128] for t in range(pairs4 // 4)]
    stack = jnp.concatenate(
        [jnp.concatenate([x[8 * dc : 8 * dc + 8] for x in tiles], axis=0) for dc in range(2)], axis=1
    )
    upper = stack.astype(BF)
    lower = (stack - upper.astype(F32)).astype(BF)
    res = dot(jnp.concatenate([upper, lower], axis=0), sel_ref[...])
    count = 8 * len(tiles)
    res = res[:count] + res[count:]
    for k in range(2):
        spill[k] = res[:, 128 * k : 128 * k + 128]
    for c in range(2):
        for dr in range(2):
            for k in range(2):
                tend[c, pl.ds(2 * k + dr, pairs4 // 2, stride=4), :] = spill[
                    k, pl.ds(dr * 2 + c, pairs4 // 2, stride=8), :
                ]
    land = land_ref[...].astype(F32)
    for c in range(2):
        total = vel_ref[c].astype(F32) + (tend[c] + b4_ref[c])
        out_ref[c] = (land * total).astype(BF)


def call(fn, ins, outs, scratch, scalars=0, flops=0, aliases=None, far_ins=()):
    vmem = pl.BlockSpec(memory_space=pltpu.VMEM)
    smem = pl.BlockSpec(memory_space=pltpu.SMEM)
    hbm = pl.BlockSpec(memory_space=pltpu.HBM)
    specs = [smem] * scalars + [vmem] * (len(ins) - scalars)
    ins = list(ins)
    for k in far_ins:
        specs[k] = hbm
        ins[k] = pltpu.with_memory_space_constraint(ins[k], pltpu.HBM)
    return pl.pallas_call(
        fn,
        out_shape=outs,
        in_specs=specs,
        out_specs=[vmem] * len(outs),
        scratch_shapes=scratch,
        input_output_aliases=aliases or {},
        cost_estimate=pl.CostEstimate(flops=flops, bytes_accessed=1 << 20, transcendentals=0),
        compiler_params=pltpu.CompilerParams(
            vmem_limit_bytes=32 << 20
        ),
    )(*ins)


def step(velocity, land_sea, fold_pivot, w1, b1, w2, b2, w3, b3, w4, b4):
    rows = velocity.shape[2]
    cols = velocity.shape[3]
    n = lax.axis_size("lon")
    vel = velocity.reshape(2, rows, cols)
    land = land_sea.reshape(rows, cols)
    w2, w3, w4 = (jnp.swapaxes(w, 2, 3) for w in (w2, w3, w4))
    b1, b2, b3 = b1[None], b2[None], b3[None]
    shape = jax.ShapeDtypeStruct
    scratch = pltpu.VMEM
    sems = pltpu.SemaphoreType.DMA
    (own,) = call(
        mask_body,
        [vel, land],
        [shape(vel.shape, BF)],
        [scratch(vel.shape, BF), scratch(land.shape, jnp.int32), sems((2,))],
        far_ins=(0, 1),
    )
    mirror = [(i, n - 1 - i) for i in range(n)]
    pairs_a = [(i, i ^ 1) for i in range(n)]
    pairs_b = [(0, 0), (n - 1, n - 1)]
    for k in range(1, n // 2):
        pairs_b += [(2 * k - 1, 2 * k), (2 * k, 2 * k - 1)]
    far = lax.ppermute(own, "lon", mirror)
    groups = (rows + 8) // 4
    pairs = (rows + 4) // 2
    sec_shape = shape((pairs * LINE + 8, 256), F32)
    south_groups = SPLIT // 2 + 1
    north_groups = groups - SPLIT // 2
    packed = (4, 5, 16, w1.shape[3])
    field = scratch((2, rows + 16, cols), F32)
    fold = scratch((2, 16, cols), F32)
    sec, w1_wide = call(
        south_body,
        [own, w1, b1, w2, b2],
        [sec_shape, shape(packed, BF)],
        [field, scratch((2, 2 * south_groups, 64, 256), BF)]
        + [scratch((2, 3, 32 * SPLIT + 8, 256), F32), scratch(packed, F32)]
        + [scratch(x.shape, x.dtype) for x in (w1, b1, w2, b2)]
        + [sems((4,))],
        flops=2 * 64 * SPLIT * 256 * 4608,
        far_ins=(1, 2, 3, 4),
    )
    both = jnp.concatenate([own, far[:, rows - 8 :]], axis=1)
    near_a = lax.ppermute(both, "lon", pairs_a)
    near_b = lax.ppermute(both, "lon", pairs_b)
    sec, w3_wide, w4_wide, sel = call(
        functools.partial(north_body, lon_count=n),
        [fold_pivot, own, far, w1_wide, b1, w2, b2, w3, w4, sec],
        [sec_shape, shape((256, 512), BF), shape((16, 512), BF), shape((256, 256), BF)],
        [field, fold, scratch((2, 2 * north_groups, 64, 256), BF)]
        + [scratch((2, 3, 32 * (pairs - SPLIT) + 8, 256), F32)],
        scalars=1,
        flops=2 * 64 * (pairs - SPLIT) * 256 * 4608,
        aliases={9: 0},
    )
    out, _ = call(
        functools.partial(last_body, lon_count=n),
        [fold_pivot, b4, vel, land, own, far, near_a, near_b]
        + [w1_wide, b1, w2, b2, w3_wide, b3, w4_wide, sel, sec],
        [shape((2, rows, cols), BF), sec_shape],
        [
            field,
            fold,
            scratch((2, 2 * groups, 2 * EDGE, 256), BF),
            scratch((3, 2 * pairs * EDGE + 8, 256), F32),
            scratch((2, 2, pairs // 2 * LINE + 8, 128), F32),
            scratch((pairs * LINE + 8, 128), F32),
            scratch((2, 64, 128), F32),
            scratch((2, rows, cols), F32),
        ],
        scalars=2,
        flops=2 * 64 * pairs * 256 * 1024,
        aliases={16: 1},
    )
    return out.reshape(velocity.shape)


def solution(mesh):
    in_specs = (
        P(None, ("members", "lev"), None, "lon"),
        P(("members", "lev"), None, "lon"),
    ) + (P(),) * 9
    out_specs = P(None, ("members", "lev"), None, "lon")
    return jax.shard_map(step, mesh=mesh, in_specs=in_specs, out_specs=out_specs, check_vma=False)
```

```python
import functools

import jax
import jax.numpy as jnp
from jax import lax
from jax.experimental import pallas as pl
from jax.experimental.pallas import tpu as pltpu
from jax.sharding import PartitionSpec as P

BF = jnp.bfloat16
F32 = jnp.float32
EDGE = 8
LINE = 72
SPLIT = 8


def dot(a, b):
    return jnp.dot(a, b, preferred_element_type=F32)


def dot_nt(a, b):
    return lax.dot_general(a, b, (((1,), (1,)), ((), ())), preferred_element_type=F32)


def iota(shape, dim):
    return lax.broadcasted_iota(jnp.int32, shape, dim)


def roll_lanes(x, shift):
    return pltpu.roll(x, shift % x.shape[1], axis=1)


def first_weights(w1_ref, row):
    zero = jnp.zeros(w1_ref.shape[2:], BF)
    sides = []
    for b in range(2):
        tiles = [w1_ref[row, t - b] if 0 <= t - b < 5 else zero for t in range(6)]
        sides.append(jnp.concatenate(tiles, axis=0))
    return jnp.concatenate(sides, axis=1)


def load_field(field_ref, values):
    rows = values[0].shape[0]
    for c in range(2):
        field_ref[c, 0:8, :] = jnp.zeros((8, values[0].shape[1]), F32)
        field_ref[c, rows : rows + 16, :] = jnp.zeros((16, values[0].shape[1]), F32)
        field_ref[c, 6 : rows + 6, :] = values[c]


def load_fold(fold_ref, tails):
    for c in range(2):
        fold_ref[c] = jnp.zeros(fold_ref.shape[1:], F32)
        for k in range(1, 7):
            fold_ref[c, 5 + k : 6 + k, :] = -tails[c][7 - k : 8 - k]


def patches(ref, start, shifted):
    tiles = []
    windows = [ref[c, start : start + 8, :] for c in range(2)]
    for t in range(6):
        tiles.append(jnp.concatenate([shifted(windows[c], t, c) for c in range(2)], axis=0))
    return jnp.concatenate(tiles, axis=0).astype(BF)


def left_sides(field_ref, fold_ref, pivot_ref, wide, pick, pick_fold, groups, rows):
    out = []
    for g in groups:
        part = dot_nt(pick, patches(field_ref, 4 * g, lambda x, t, c: roll_lanes(x, -t)))
        if 4 * g + 8 > rows + 6:
            ups = [pivot_ref[c] - (wide - 1) > 0 for c in range(2)]

            def turned(x, t, c):
                return jnp.where(ups[c], roll_lanes(x, t - 1), roll_lanes(x, t + 1))

            part = part + dot_nt(pick_fold, patches(fold_ref, 4 * g - rows, turned))
        out.append(part)
    return out


def second_weights(w2_ref):
    zero = jnp.zeros(w2_ref.shape[2:], BF)
    rows = []
    for shift in range(3):
        for dr in range(2):
            for dc in range(2):
                cells = []
                for a in range(6):
                    for b in (2 * shift - dc, 2 * shift + 1 - dc):
                        inside = 0 <= a - dr < 5 and 0 <= b < 5
                        cells.append(w2_ref[a - dr, b] if inside else zero)
                rows.append(jnp.concatenate(cells, axis=1))
    return jnp.concatenate(rows, axis=0)


def block_weights(w_ref, shifts):
    zero = jnp.zeros(w_ref.shape[2:], F32)
    rows = []
    for dr in range(2):
        for dc in range(2):
            cells = []
            for er in range(2):
                for ec in shifts:
                    for r in range(2):
                        for c in range(2):
                            a, b = 2 * er + r - dr, 2 * ec + c - dc
                            inside = 0 <= a < 3 and 0 <= b < 3
                            cells.append(w_ref[a, b].astype(F32) if inside else zero)
            rows.append(jnp.concatenate(cells, axis=1))
    return rows


def edge_tile(values, blocks):
    lane = iota(values[0].shape, 1) >> 4
    tile = jnp.zeros(values[0].shape, F32)
    for value, block in zip(values, blocks):
        tile = jnp.where(lane == block, roll_lanes(value, 8 + 16 * block), tile)
    return tile


def mask_body(
    vel_hbm, land_hbm, w1_hbm, b1_hbm, b2_hbm, own_ref, pay_ref, w1_ref, b1_ref, b2_ref,
    vel_ref, land_ref, sems,
):
    moves = [(vel_hbm, vel_ref), (land_hbm, land_ref)]
    moves += [(w1_hbm, w1_ref), (b1_hbm, b1_ref), (b2_hbm, b2_ref)]
    copies = [pltpu.make_async_copy(a, b, sems.at[k]) for k, (a, b) in enumerate(moves)]
    for copy in copies:
        copy.start()
    for copy in copies[:2]:
        copy.wait()
    land = land_ref[...].astype(F32)
    own = [vel_ref[c].astype(F32) * land for c in range(2)]
    for c in range(2):
        own_ref[c] = own[c].astype(BF)
    rows = land.shape[0]
    tiles = [own[c][rows - 8 :] for c in range(2)]
    cuts = [own[c][k : k + 8] for c in range(2) for k in range(0, rows, 8)]
    tiles.append(edge_tile(cuts, range(len(cuts))))
    pay_ref[...] = jnp.concatenate(tiles, axis=0).astype(BF)
    for copy in copies[2:]:
        copy.wait()


def pair_body(pay_ref, far_ref, both_ref):
    far = far_ref[...].astype(F32)
    half = far.shape[1] // 32
    tile = edge_tile([far[0:8], far[8:16]], (half - 1, 2 * half - 1))
    own = pay_ref[...].astype(F32)[16:24]
    both_ref[...] = jnp.concatenate([own, tile], axis=0).astype(BF)


def pack_first(w1_ref, wide_ref, w1_out):
    wide_ref[...] = jnp.zeros_like(wide_ref)
    for t in range(5):
        for a in range(5):
            value = w1_ref[a, t].astype(F32)
            for row in range(4):
                for c in range(2):
                    at = 8 * c + row + a
                    wide_ref[row, t, at : at + 1, :] = value[c : c + 1]
    w1_out[...] = wide_ref[...].astype(BF)


def first_layer(lefts, f_ref, w1_ref, bias):
    stacked = jnp.concatenate(lefts, axis=0).astype(BF)
    size = lefts[0].shape[0]
    for row in range(4):
        res = dot(stacked, first_weights(w1_ref, row))
        res = jnp.maximum(res + bias, 0.0).astype(BF)
        for g in range(len(lefts)):
            f_ref[row % 2, 2 * g + row // 2] = res[size * g : size * g + size]


def second_layer(f_ref, right, acc_ref, lo, count):
    size = f_ref.shape[2]
    left = jnp.concatenate(
        [
            f_ref[a % 2, lo + a // 2 : lo + a // 2 + count].reshape(count * size, 256)
            for a in range(6)
        ],
        axis=1,
    )
    res = dot_nt(left, right)
    for shift in range(3):
        acc_ref[shift, 0 : count * size, :] = res[:, 256 * shift : 256 * shift + 256]


def shifted_sum(acc_ref, at, size, bias):
    parts = [acc_ref[k, at + k : at + k + size, :] for k in range(acc_ref.shape[0])]
    total = parts[0]
    for part in parts[1:]:
        total = total + part
    return jnp.maximum(total + bias, 0.0)


def inner_second(f_ref, right, bias, acc_ref, sec_ref, start, count):
    chunks = acc_ref.shape[0]
    step = count // chunks
    for k in range(chunks):
        second_layer(f_ref, right, acc_ref.at[k], k * step, step)
        for p in range(step):
            at = (start + k * step + p) * LINE
            sec_ref[at : at + 64, :] = shifted_sum(acc_ref.at[k], 64 * p, 64, bias)


def inner_picks(cols):
    lane = iota((64, cols), 1)
    slot = iota((64, cols), 0)
    fold = lax.rem(2 * cols + 5 - 2 * slot, cols)
    return (lane == 2 * slot - 6).astype(BF), (lane == fold).astype(BF)


def south_body(
    own_ref, w1_ref, b1_ref, w2_hbm, b2_ref, sec, w1_out, field, f, acc, wide, w2_ref, sem
):
    copy = pltpu.make_async_copy(w2_hbm, w2_ref, sem)
    copy.start()
    pack_first(w1_ref, wide, w1_out)
    rows = own_ref.shape[1]
    cols = own_ref.shape[2]
    load_field(field, [own_ref[c].astype(F32) for c in range(2)])
    pick, _ = inner_picks(cols)
    lefts = left_sides(field, None, None, 0, pick, None, range(SPLIT // 2 + 1), rows)
    first_layer(lefts, f, w1_out, jnp.concatenate([b1_ref[...]] * 2, axis=1))
    copy.wait()
    bias2 = jnp.concatenate([b2_ref[...]] * 4, axis=1)
    inner_second(f, second_weights(w2_ref), bias2, acc, sec, 0, SPLIT)


def north_body(
    pivot_ref, own_ref, far_ref, w1_ref, b1_ref, w2_ref, b2_ref, w3_ref, w4_ref, sec_in,
    sec, w3_out, w4_out, sel_out, field, fold, f, acc, *, lon_count,
):
    bias1 = jnp.concatenate([b1_ref[...]] * 2, axis=1)
    bias2 = jnp.concatenate([b2_ref[...]] * 4, axis=1)
    rows = own_ref.shape[1]
    cols = own_ref.shape[2]
    blocks = block_weights(w3_ref, (0,)) + block_weights(w3_ref, (1,))
    w3_out[...] = jnp.concatenate(blocks, axis=0).astype(BF)
    tiny = block_weights(w4_ref, (0, 1))
    blank = jnp.zeros((4, tiny[0].shape[1]), F32)
    order = [tiny[0], tiny[2], blank, tiny[1], tiny[3], blank]
    w4_out[...] = jnp.concatenate(order, axis=0).astype(BF)
    src = iota((256, 256), 0)
    want = 2 * (src & 127) + (src >> 7)
    sel_out[...] = (iota((256, 256), 1) == want).astype(BF)
    load_field(field, [own_ref[c].astype(F32) for c in range(2)])
    far = far_ref[...].astype(F32)
    load_fold(fold, [far[8 * c : 8 * c + 8] for c in range(2)])
    pick, pick_fold = inner_picks(cols)
    groups = range(SPLIT // 2, (rows + 8) // 4)
    lefts = left_sides(field, fold, pivot_ref, lon_count * cols, pick, pick_fold, groups, rows)
    first_layer(lefts, f, w1_ref, bias1)
    count = (rows + 4) // 2 - SPLIT
    inner_second(f, second_weights(w2_ref), bias2, acc, sec, SPLIT, count)


def last_body(
    pivot_ref, b4_ref, vel_ref, land_ref, own_ref, pay_ref, far_ref, near_a_ref, near_b_ref,
    w1_ref, b1_ref, w2_ref, b2_ref, w3_ref, b3_ref, w4_ref, sel_ref, sec_in,
    out_ref, sec, field, fold, f, acc, acc3, third, spill, tend, *, lon_count,
):
    rows = own_ref.shape[1]
    cols = own_ref.shape[2]
    bias1 = jnp.concatenate([b1_ref[...]] * 2, axis=1)
    bias2 = jnp.concatenate([b2_ref[...]] * 4, axis=1)
    bias3 = jnp.concatenate([b3_ref[...]] * 4, axis=1)
    groups = (rows + 8) // 4
    pairs = (rows + 4) // 2

    lon = lax.axis_index("lon")
    even = lax.rem(lon, 2) == 0
    own = own_ref[...].astype(F32)
    far = far_ref[...].astype(F32)
    wrap = jnp.concatenate([far[16:24], pay_ref[...].astype(F32)[16:24]], axis=0)
    near_a = near_a_ref[...].astype(F32)
    near_b = near_b_ref[...].astype(F32)
    west = jnp.where(lon == 0, wrap, jnp.where(even, near_b, near_a))
    east = jnp.where(lon == lon_count - 1, wrap, jnp.where(even, near_a, near_b))
    lane = iota((8, cols), 1)
    half = cols // 2

    def around(mid, after, before, block):
        outer = jnp.where(
            lane < half // 2,
            roll_lanes(after, -16 * block - 8),
            roll_lanes(before, half - 8 - 16 * block),
        )
        inner = jnp.where(lane < half + half // 2, roll_lanes(mid, half), mid)
        return jnp.where(lane < half, outer, inner)

    wide = []
    tails = []
    for c in range(2):
        parts = []
        for k in range(rows // 8):
            block = c * (rows // 8) + k
            parts.append(around(own[c, 8 * k : 8 * k + 8], east[0:8], west[0:8], block))
        wide.append(jnp.concatenate(parts, axis=0))
        tails.append(around(far[8 * c : 8 * c + 8], west[8:16], east[8:16], block))
    load_field(field, wide)
    load_fold(fold, tails)
    slot = iota((2 * EDGE, cols), 0)
    lane = iota((2 * EDGE, cols), 1)
    low = slot < EDGE
    pair = jnp.where(low, slot, slot + (cols // 2 - 2 - EDGE))
    start = 2 * pair - 6 + jnp.where(low, cols // 2, 0)
    pick = (lane == lax.rem(start + cols, cols)).astype(BF)
    start = cols + 5 - 2 * pair + jnp.where(low, 0, cols // 2)
    pick_fold = (lane == lax.rem(start + cols, cols)).astype(BF)
    lefts = left_sides(
        field, fold, pivot_ref, lon_count * cols, pick, pick_fold, range(groups), rows
    )
    first_layer(lefts, f, w1_ref, bias1)
    second_layer(f, second_weights(w2_ref), acc, 0, pairs)
    line = iota((EDGE, 256), 0)
    for k in range(pairs):
        at = k * LINE
        new = shifted_sum(acc, 2 * EDGE * k, EDGE, bias2)
        sec[at : at + 8, :] = jnp.where(line < 4, new, sec_in[at : at + 8, :])
        new = pltpu.roll(shifted_sum(acc, 2 * EDGE * k + EDGE, EDGE, bias2), 6, axis=0)
        sec[at + 56 : at + 64, :] = jnp.where(line >= 6, new, sec_in[at + 56 : at + 64, :])
        sec[at + 64 : at + 72, :] = new

    pairs3 = pairs - 1
    right = w3_ref[...]
    middle = (pairs3 + 1) // 2
    for part, (lo, hi) in enumerate(((0, middle), (middle, pairs3))):
        base, size = lo * LINE, (hi - lo) * LINE
        left = [sec[base + at : base + at + size, :].astype(BF) for at in (0, LINE)]
        res = dot_nt(jnp.concatenate(left, axis=1), right)
        for shift in range(2):
            acc3[part, shift, 0:size, :] = res[:, 128 * shift : 128 * shift + 128]
        third[base : base + size, :] = shifted_sum(acc3.at[part], 0, size, bias3)

    pairs4 = pairs - 2
    right = w4_ref[...]
    tiles = []
    for lo in (0, pairs4 // 2):
        left = jnp.concatenate(
            [
                jnp.concatenate(
                    [
                        third[k * LINE + at : k * LINE + at + 64, :]
                        for k in range(lo, lo + pairs4 // 2)
                    ],
                    axis=0,
                ).astype(BF)
                for at in (0, 1, LINE, LINE + 1)
            ],
            axis=1,
        )
        res = dot_nt(right, left)
        tiles += [res[:, 128 * t : 128 * t + 128] for t in range(pairs4 // 4)]
    stack = jnp.concatenate(
        [jnp.concatenate([x[8 * dc : 8 * dc + 8] for x in tiles], axis=0) for dc in range(2)], axis=1
    )
    upper = stack.astype(BF)
    lower = (stack - upper.astype(F32)).astype(BF)
    res = dot(jnp.concatenate([upper, lower], axis=0), sel_ref[...])
    count = 8 * len(tiles)
    res = res[:count] + res[count:]
    for k in range(2):
        spill[k] = res[:, 128 * k : 128 * k + 128]
    for c in range(2):
        for dr in range(2):
            for k in range(2):
                tend[c, pl.ds(2 * k + dr, pairs4 // 2, stride=4), :] = spill[
                    k, pl.ds(dr * 2 + c, pairs4 // 2, stride=8), :
                ]
    land = land_ref[...].astype(F32)
    for c in range(2):
        total = vel_ref[c].astype(F32) + (tend[c] + b4_ref[c])
        out_ref[c] = (land * total).astype(BF)


def call(fn, ins, outs, scratch, scalars=0, flops=0, aliases=None, far_ins=()):
    vmem = pl.BlockSpec(memory_space=pltpu.VMEM)
    smem = pl.BlockSpec(memory_space=pltpu.SMEM)
    hbm = pl.BlockSpec(memory_space=pltpu.HBM)
    specs = [smem] * scalars + [vmem] * (len(ins) - scalars)
    ins = list(ins)
    for k in far_ins:
        specs[k] = hbm
        ins[k] = pltpu.with_memory_space_constraint(ins[k], pltpu.HBM)
    return pl.pallas_call(
        fn,
        out_shape=outs,
        in_specs=specs,
        out_specs=[vmem] * len(outs),
        scratch_shapes=scratch,
        input_output_aliases=aliases or {},
        cost_estimate=pl.CostEstimate(flops=flops, bytes_accessed=1 << 20, transcendentals=0),
        compiler_params=pltpu.CompilerParams(
            vmem_limit_bytes=32 << 20
        ),
    )(*ins)


def step(velocity, land_sea, fold_pivot, w1, b1, w2, b2, w3, b3, w4, b4):
    rows = velocity.shape[2]
    cols = velocity.shape[3]
    n = lax.axis_size("lon")
    vel = velocity.reshape(2, rows, cols)
    land = land_sea.reshape(rows, cols)
    w2, w3, w4 = (jnp.swapaxes(w, 2, 3) for w in (w2, w3, w4))
    b1, b2, b3 = b1[None], b2[None], b3[None]
    shape = jax.ShapeDtypeStruct
    scratch = pltpu.VMEM
    sems = pltpu.SemaphoreType.DMA
    own, pay, w1, b1, b2 = call(
        mask_body,
        [vel, land, w1, b1, b2],
        [shape(vel.shape, BF), shape((24, cols), BF)]
        + [shape(x.shape, x.dtype) for x in (w1, b1, b2)],
        [scratch(vel.shape, BF), scratch(land.shape, jnp.int32), sems((5,))],
        far_ins=(0, 1, 2, 3, 4),
    )
    mirror = [(i, n - 1 - i) for i in range(n)]
    pairs_a = [(i, i ^ 1) for i in range(n)]
    levels = lax.axis_size("lev")
    pairs_b = []
    for level in range(levels):
        for k in range(1, n // 2):
            low, high = (2 * k - 1) * levels + level, 2 * k * levels + level
            pairs_b += [(low, high), (high, low)]
        for end in (0, n - 1):
            pairs_b.append((end * levels + level, end * levels + (level + 1) % levels))
    far = lax.ppermute(pay, "lon", mirror)
    groups = (rows + 8) // 4
    pairs = (rows + 4) // 2
    sec_shape = shape((pairs * LINE + 8, 256), F32)
    south_groups = SPLIT // 2 + 1
    north_groups = groups - SPLIT // 2
    packed = (4, 5, 16, w1.shape[3])
    field = scratch((2, rows + 16, cols), F32)
    fold = scratch((2, 16, cols), F32)
    sec, w1_wide = call(
        south_body,
        [own, w1, b1, w2, b2],
        [sec_shape, shape(packed, BF)],
        [field, scratch((2, 2 * south_groups, 64, 256), BF)]
        + [scratch((2, 3, 32 * SPLIT + 8, 256), F32), scratch(packed, F32)]
        + [scratch(w2.shape, BF), sems(())],
        flops=2 * 64 * SPLIT * 256 * 4608,
        far_ins=(3,),
    )
    (both,) = call(pair_body, [pay, far], [shape((16, cols), BF)], [])
    near_a = lax.ppermute(both, "lon", pairs_a)
    near_b = lax.ppermute(both, ("lon", "lev"), pairs_b)
    sec, w3_wide, w4_wide, sel = call(
        functools.partial(north_body, lon_count=n),
        [fold_pivot, own, far, w1_wide, b1, w2, b2, w3, w4, sec],
        [sec_shape, shape((256, 512), BF), shape((16, 512), BF), shape((256, 256), BF)],
        [field, fold, scratch((2, 2 * north_groups, 64, 256), BF)]
        + [scratch((2, 3, 32 * (pairs - SPLIT) + 8, 256), F32)],
        scalars=1,
        flops=2 * 64 * (pairs - SPLIT) * 256 * 4608,
        aliases={9: 0},
    )
    out, _ = call(
        functools.partial(last_body, lon_count=n),
        [fold_pivot, b4, vel, land, own, pay, far, near_a, near_b]
        + [w1_wide, b1, w2, b2, w3_wide, b3, w4_wide, sel, sec],
        [shape((2, rows, cols), BF), sec_shape],
        [
            field,
            fold,
            scratch((2, 2 * groups, 2 * EDGE, 256), BF),
            scratch((3, 2 * pairs * EDGE + 8, 256), F32),
            scratch((2, 2, pairs // 2 * LINE + 8, 128), F32),
            scratch((pairs * LINE + 8, 128), F32),
            scratch((2, 64, 128), F32),
            scratch((2, rows, cols), F32),
        ],
        scalars=2,
        flops=2 * 64 * pairs * 256 * 1024,
        aliases={17: 1},
    )
    return out.reshape(velocity.shape)


def solution(mesh):
    in_specs = (
        P(None, ("members", "lev"), None, "lon"),
        P(("members", "lev"), None, "lon"),
    ) + (P(),) * 9
    out_specs = P(None, ("members", "lev"), None, "lon")
    return jax.shard_map(step, mesh=mesh, in_specs=in_specs, out_specs=out_specs, check_vma=False)
```

```python
import functools

import jax
import jax.numpy as jnp
from jax import lax
from jax.experimental import pallas as pl
from jax.experimental.pallas import tpu as pltpu
from jax.sharding import PartitionSpec as P

BF = jnp.bfloat16
F32 = jnp.float32
EDGE = 8
LINE = 80
SPLIT = 6


def dot(a, b):
    return jnp.dot(a, b, preferred_element_type=F32)


def dot_nt(a, b):
    return lax.dot_general(a, b, (((1,), (1,)), ((), ())), preferred_element_type=F32)


def iota(shape, dim):
    return lax.broadcasted_iota(jnp.int32, shape, dim)


def roll_lanes(x, shift):
    return pltpu.roll(x, shift % x.shape[1], axis=1)


def first_weights(w1_ref, row):
    zero = jnp.zeros(w1_ref.shape[2:], BF)
    sides = []
    for b in range(2):
        tiles = [w1_ref[row, t - b] if 0 <= t - b < 5 else zero for t in range(6)]
        sides.append(jnp.concatenate(tiles, axis=0))
    return jnp.concatenate(sides, axis=1)


def load_field(field_ref, values):
    rows = values[0].shape[0]
    for c in range(2):
        field_ref[c, 0:8, :] = jnp.zeros((8, values[0].shape[1]), F32)
        field_ref[c, rows : rows + 16, :] = jnp.zeros((16, values[0].shape[1]), F32)
        field_ref[c, 6 : rows + 6, :] = values[c]


def load_fold(fold_ref, tails):
    for c in range(2):
        fold_ref[c] = jnp.zeros(fold_ref.shape[1:], F32)
        for k in range(1, 7):
            fold_ref[c, 5 + k : 6 + k, :] = -tails[c][7 - k : 8 - k]


def patches(ref, start, shifted):
    tiles = []
    windows = [ref[c, start : start + 8, :] for c in range(2)]
    for t in range(6):
        tiles.append(jnp.concatenate([shifted(windows[c], t, c) for c in range(2)], axis=0))
    return jnp.concatenate(tiles, axis=0).astype(BF)


def left_sides(field_ref, fold_ref, pivot_ref, wide, pick, pick_fold, groups, rows):
    out = []
    for g in groups:
        part = dot_nt(pick, patches(field_ref, 4 * g, lambda x, t, c: roll_lanes(x, -t)))
        if 4 * g + 8 > rows + 6:
            ups = [
                jnp.broadcast_to(pivot_ref[:, c : c + 1], (8, pick.shape[1])) > wide - 1
                for c in range(2)
            ]

            def turned(x, t, c):
                return jnp.where(ups[c], roll_lanes(x, t - 1), roll_lanes(x, t + 1))

            part = part + dot_nt(pick_fold, patches(fold_ref, 4 * g - rows, turned))
        out.append(part)
    return out


def second_weights(w2_ref):
    zero = jnp.zeros(w2_ref.shape[2:], BF)
    rows = []
    for shift in range(3):
        for dr in range(2):
            for dc in range(2):
                cells = []
                for a in range(6):
                    for b in (2 * shift - dc, 2 * shift + 1 - dc):
                        inside = 0 <= a - dr < 5 and 0 <= b < 5
                        cells.append(w2_ref[a - dr, b] if inside else zero)
                rows.append(jnp.concatenate(cells, axis=1))
    return jnp.concatenate(rows, axis=0)


def block_weights(w_ref, shifts):
    zero = jnp.zeros(w_ref.shape[2:], F32)
    rows = []
    for dr in range(2):
        for dc in range(2):
            cells = []
            for er in range(2):
                for ec in shifts:
                    for r in range(2):
                        for c in range(2):
                            a, b = 2 * er + r - dr, 2 * ec + c - dc
                            inside = 0 <= a < 3 and 0 <= b < 3
                            cells.append(w_ref[a, b].astype(F32) if inside else zero)
            rows.append(jnp.concatenate(cells, axis=1))
    return rows


def edge_tile(values, blocks):
    lane = iota(values[0].shape, 1) >> 4
    tile = jnp.zeros(values[0].shape, F32)
    for value, block in zip(values, blocks):
        tile = jnp.where(lane == block, roll_lanes(value, 8 + 16 * block), tile)
    return tile


def mask_body(*refs, small):
    vel_hbm, land_hbm = refs[:2]
    own_ref, pay_ref = refs[2 + small : 4 + small]
    vel_ref, land_ref, sems = refs[4 + 2 * small :]
    moves = [(vel_hbm, vel_ref), (land_hbm, land_ref)]
    moves += list(zip(refs[2 : 2 + small], refs[4 + small : 4 + 2 * small]))
    copies = [pltpu.make_async_copy(a, b, sems.at[k]) for k, (a, b) in enumerate(moves)]
    for copy in copies:
        copy.start()
    for copy in copies[:2]:
        copy.wait()
    land = land_ref[...].astype(F32)
    own = [vel_ref[c].astype(F32) * land for c in range(2)]
    for c in range(2):
        own_ref[c] = own[c].astype(BF)
    rows = land.shape[0]
    tiles = [own[c][rows - 8 :] for c in range(2)]
    cuts = [own[c][k : k + 8] for c in range(2) for k in range(0, rows, 8)]
    tiles.append(edge_tile(cuts, range(len(cuts))))
    pay_ref[...] = jnp.concatenate(tiles, axis=0).astype(BF)
    for copy in copies[2:]:
        copy.wait()


def pair_body(pay_ref, far_ref, both_ref):
    far = far_ref[...].astype(F32)
    half = far.shape[1] // 32
    tile = edge_tile([far[0:8], far[8:16]], (half - 1, 2 * half - 1))
    own = pay_ref[...].astype(F32)[16:24]
    both_ref[...] = jnp.concatenate([own, tile], axis=0).astype(BF)


def pack_first(w1_ref, wide_ref, w1_out):
    wide_ref[...] = jnp.zeros_like(wide_ref)
    for t in range(5):
        for a in range(5):
            value = w1_ref[a, t].astype(F32)
            for c in range(2):
                wide_ref[t, c, a : a + 1, :] = value[c : c + 1]
    for t in range(5):
        base = [wide_ref[t, c] for c in range(2)]
        for row in range(4):
            both = [pltpu.roll(x, row, axis=0) if row else x for x in base]
            w1_out[row, t] = jnp.concatenate(both, axis=0).astype(BF)


def first_layer(lefts, f_ref, w1_ref, bias, start=0):
    stacked = jnp.concatenate(lefts, axis=0).astype(BF)
    size = lefts[0].shape[0]
    for row in range(4):
        res = dot(stacked, first_weights(w1_ref, row))
        res = jnp.maximum(res + bias, 0.0).astype(BF)
        for g in range(len(lefts)):
            f_ref[row % 2, 2 * (start + g) + row // 2] = res[size * g : size * g + size]


def second_layer(f_ref, right, acc_ref, lo, count):
    size = f_ref.shape[2]
    left = jnp.concatenate(
        [
            f_ref[a % 2, lo + a // 2 : lo + a // 2 + count].reshape(count * size, 256)
            for a in range(6)
        ],
        axis=1,
    )
    res = dot_nt(left, right)
    for shift in range(3):
        acc_ref[shift, 0 : count * size, :] = res[:, 256 * shift : 256 * shift + 256]


def shifted_sum(acc_ref, at, size, bias):
    parts = [acc_ref[k, at + k : at + k + size, :] for k in range(acc_ref.shape[0])]
    total = parts[0]
    for part in parts[1:]:
        total = total + part
    return jnp.maximum(total + bias, 0.0)


def inner_second(f_ref, right, bias, acc_ref, sec_ref, start, count):
    chunks = acc_ref.shape[0]
    step = count // chunks
    for k in range(chunks):
        second_layer(f_ref, right, acc_ref.at[k], start + k * step, step)
        for p in range(step):
            at = (start + k * step + p) * LINE
            sec_ref[at : at + 64, :] = shifted_sum(acc_ref.at[k], 64 * p, 64, bias).astype(BF)


def inner_picks(cols):
    lane = iota((64, cols), 1)
    slot = iota((64, cols), 0)
    fold = lax.rem(2 * cols + 5 - 2 * slot, cols)
    return (lane == 2 * slot - 6).astype(BF), (lane == fold).astype(BF)


def south_body(
    own_ref, w1_ref, b1_ref, w2_hbm, b2_ref, sec, w1_out, f, field, acc, wide, w2_ref, sem
):
    copy = pltpu.make_async_copy(w2_hbm, w2_ref, sem)
    copy.start()
    pack_first(w1_ref, wide, w1_out)
    rows = own_ref.shape[1]
    cols = own_ref.shape[2]
    load_field(field, [own_ref[c].astype(F32) for c in range(2)])
    pick, _ = inner_picks(cols)
    lefts = left_sides(field, None, None, 0, pick, None, range((rows - 2) // 4 + 1), rows)
    first_layer(lefts, f, w1_out, jnp.concatenate([b1_ref[...]] * 2, axis=1))
    copy.wait()
    bias2 = jnp.concatenate([b2_ref[...]] * 4, axis=1)
    inner_second(f, second_weights(w2_ref), bias2, acc, sec, 0, SPLIT)


def north_body(
    pivot_ref, own_ref, far_ref, w1_ref, b1_ref, w2_ref, b2_ref, w3_ref, w4_ref, sec_in,
    f_in, sec, w3_out, w4_out, sel_out, f, field, fold, acc, *, lon_count,
):
    bias1 = jnp.concatenate([b1_ref[...]] * 2, axis=1)
    bias2 = jnp.concatenate([b2_ref[...]] * 4, axis=1)
    rows = own_ref.shape[1]
    cols = own_ref.shape[2]
    blocks = block_weights(w3_ref, (0,)) + block_weights(w3_ref, (1,))
    w3_out[...] = jnp.concatenate(blocks, axis=0).astype(BF)
    tiny = block_weights(w4_ref, (0, 1))
    blank = jnp.zeros((4, tiny[0].shape[1]), F32)
    order = [tiny[0], tiny[2], blank, tiny[1], tiny[3], blank]
    w4_out[...] = jnp.concatenate(order, axis=0).astype(BF)
    src = iota((256, 256), 0)
    want = 2 * (src & 127) + (src >> 7)
    sel_out[...] = (iota((256, 256), 1) == want).astype(BF)
    load_field(field, [own_ref[c].astype(F32) for c in range(2)])
    far = far_ref[...].astype(F32)
    load_fold(fold, [far[8 * c : 8 * c + 8] for c in range(2)])
    pick, pick_fold = inner_picks(cols)
    groups = range((rows - 2) // 4 + 1, (rows + 8) // 4)
    lefts = left_sides(field, fold, pivot_ref, lon_count * cols, pick, pick_fold, groups, rows)
    first_layer(lefts, f, w1_ref, bias1, groups[0])
    count = (rows + 4) // 2 - SPLIT
    inner_second(f, second_weights(w2_ref), bias2, acc, sec, SPLIT, count)


def last_body(
    pivot_ref, lon_ref, b4_ref, vel_ref, land_ref, own_ref, pay_ref, far_ref, near_a_ref, near_b_ref,
    w1_ref, b1_ref, w2_ref, b2_ref, w3_ref, b3_ref, w4_ref, sel_ref, sec_in,
    out_ref, sec, field, fold, f, acc, acc3, third, spill, tend, *, lon_count,
):
    rows = own_ref.shape[1]
    cols = own_ref.shape[2]
    bias1 = jnp.concatenate([b1_ref[...]] * 2, axis=1)
    bias2 = jnp.concatenate([b2_ref[...]] * 4, axis=1)
    bias3 = jnp.concatenate([b3_ref[...]] * 4, axis=1)
    groups = (rows + 8) // 4
    pairs = (rows + 4) // 2

    lon = jnp.broadcast_to(lon_ref[...], (16, cols))
    even = (lon & 1) == 0
    own = own_ref[...].astype(F32)
    far = far_ref[...].astype(F32)
    wrap = jnp.concatenate([far[16:24], pay_ref[...].astype(F32)[16:24]], axis=0)
    near_a = near_a_ref[...].astype(F32)
    near_b = near_b_ref[...].astype(F32)
    west = jnp.where(lon == 0, wrap, jnp.where(even, near_b, near_a))
    east = jnp.where(lon == lon_count - 1, wrap, jnp.where(even, near_a, near_b))
    lane = iota((8, cols), 1)
    half = cols // 2

    def around(mid, after, before, block):
        outer = jnp.where(
            lane < half // 2,
            roll_lanes(after, -16 * block - 8),
            roll_lanes(before, half - 8 - 16 * block),
        )
        inner = jnp.where(lane < half + half // 2, roll_lanes(mid, half), mid)
        return jnp.where(lane < half, outer, inner)

    wide = []
    tails = []
    for c in range(2):
        parts = []
        for k in range(rows // 8):
            block = c * (rows // 8) + k
            parts.append(around(own[c, 8 * k : 8 * k + 8], east[0:8], west[0:8], block))
        wide.append(jnp.concatenate(parts, axis=0))
        tails.append(around(far[8 * c : 8 * c + 8], west[8:16], east[8:16], block))
    load_field(field, wide)
    load_fold(fold, tails)
    slot = iota((2 * EDGE, cols), 0)
    lane = iota((2 * EDGE, cols), 1)
    low = slot < EDGE
    pair = jnp.where(low, slot, slot + (cols // 2 - 2 - EDGE))
    start = 2 * pair - 6 + jnp.where(low, cols // 2, 0)
    pick = (lane == lax.rem(start + cols, cols)).astype(BF)
    start = cols + 5 - 2 * pair + jnp.where(low, 0, cols // 2)
    pick_fold = (lane == lax.rem(start + cols, cols)).astype(BF)
    lefts = left_sides(
        field, fold, pivot_ref, lon_count * cols, pick, pick_fold, range(groups), rows
    )
    first_layer(lefts, f, w1_ref, bias1)
    second_layer(f, second_weights(w2_ref), acc, 0, pairs)
    line = iota((2 * EDGE, 256), 0)
    for k in range(pairs):
        at = k * LINE
        new = shifted_sum(acc, 2 * EDGE * k, 2 * EDGE, bias2)
        old = sec_in[at : at + 16, :].astype(F32)
        sec[at : at + 16, :] = jnp.where(line < 4, new, old).astype(BF)
        new = pltpu.roll(new, 6, axis=0)
        old = sec_in[at + 48 : at + 64, :].astype(F32)
        sec[at + 48 : at + 64, :] = jnp.where(line >= 14, new, old).astype(BF)
        sec[at + 64 : at + 80, :] = new.astype(BF)

    pairs3 = pairs - 1
    right = w3_ref[...]
    middle = (pairs3 + 1) // 2
    for part, (lo, hi) in enumerate(((0, middle), (middle, pairs3))):
        base, size = lo * LINE, (hi - lo) * LINE
        left = [sec[base + at : base + at + size, :] for at in (0, LINE)]
        res = dot_nt(jnp.concatenate(left, axis=1), right)
        for shift in range(2):
            acc3[part, shift, 0:size, :] = res[:, 128 * shift : 128 * shift + 128]
        for shift in range(2):
            value = shifted_sum(acc3.at[part], shift, size, bias3)
            third[shift, base : base + size, :] = value.astype(BF)

    pairs4 = pairs - 2
    right = w4_ref[...]
    tiles = []
    for lo in (0, pairs4 // 2):
        left = jnp.concatenate(
            [
                jnp.concatenate(
                    [
                        third[shift, k * LINE : k * LINE + 64, :]
                        for k in range(lo + up, lo + up + pairs4 // 2)
                    ],
                    axis=0,
                )
                for up in range(2)
                for shift in range(2)
            ],
            axis=1,
        )
        res = dot_nt(right, left)
        tiles += [res[:, 128 * t : 128 * t + 128] for t in range(pairs4 // 4)]
    stack = jnp.concatenate(
        [jnp.concatenate([x[8 * dc : 8 * dc + 8] for x in tiles], axis=0) for dc in range(2)], axis=1
    )
    upper = stack.astype(BF)
    lower = (stack - upper.astype(F32)).astype(BF)
    res = dot(jnp.concatenate([upper, lower], axis=0), sel_ref[...])
    count = 8 * len(tiles)
    res = res[:count] + res[count:]
    for k in range(2):
        spill[k] = res[:, 128 * k : 128 * k + 128]
    for c in range(2):
        for dr in range(2):
            for k in range(2):
                tend[c, pl.ds(2 * k + dr, pairs4 // 2, stride=4), :] = spill[
                    k, pl.ds(dr * 2 + c, pairs4 // 2, stride=8), :
                ]
    land = land_ref[...].astype(F32)
    for c in range(2):
        bias4 = jnp.broadcast_to(b4_ref[:, c : c + 1], (1, cols))
        total = vel_ref[c].astype(F32) + (tend[c] + bias4)
        out_ref[c] = (land * total).astype(BF)


def call(fn, ins, outs, scratch, flops=0, aliases=None, far_ins=()):
    vmem = pl.BlockSpec(memory_space=pltpu.VMEM)
    hbm = pl.BlockSpec(memory_space=pltpu.HBM)
    specs = [vmem] * len(ins)
    ins = list(ins)
    for k in far_ins:
        specs[k] = hbm
        ins[k] = pltpu.with_memory_space_constraint(ins[k], pltpu.HBM)
    return pl.pallas_call(
        fn,
        out_shape=outs,
        in_specs=specs,
        out_specs=[vmem] * len(outs),
        scratch_shapes=scratch,
        input_output_aliases=aliases or {},
        cost_estimate=pl.CostEstimate(flops=flops, bytes_accessed=1 << 20, transcendentals=0),
        compiler_params=pltpu.CompilerParams(
            vmem_limit_bytes=32 << 20
        ),
    )(*ins)


def step(velocity, land_sea, fold_pivot, w1, b1, w2, b2, w3, b3, w4, b4):
    rows = velocity.shape[2]
    cols = velocity.shape[3]
    n = lax.axis_size("lon")
    lon = jnp.full((1, 1), lax.axis_index("lon"), jnp.int32)
    vel = velocity.reshape(2, rows, cols)
    land = land_sea.reshape(rows, cols)
    w2, w3, w4 = (jnp.swapaxes(w, 2, 3) for w in (w2, w3, w4))
    b1, b2, b3, b4, fold_pivot = (x[None] for x in (b1, b2, b3, b4, fold_pivot))
    shape = jax.ShapeDtypeStruct
    scratch = pltpu.VMEM
    sems = pltpu.SemaphoreType.DMA
    near = [w1, b1, b2, b3, b4, fold_pivot]
    own, pay, w1, b1, b2, b3, b4, fold_pivot = call(
        functools.partial(mask_body, small=len(near)),
        [vel, land] + near,
        [shape(vel.shape, BF), shape((24, cols), BF)] + [shape(x.shape, x.dtype) for x in near],
        [scratch(vel.shape, BF), scratch(land.shape, jnp.int32), sems((2 + len(near),))],
        far_ins=range(2 + len(near)),
    )
    mirror = [(i, n - 1 - i) for i in range(n)]
    pairs_a = [(i, i ^ 1) for i in range(n)]
    levels = lax.axis_size("lev")
    pairs_b = []
    for level in range(levels):
        for k in range(1, n // 2):
            low, high = (2 * k - 1) * levels + level, 2 * k * levels + level
            pairs_b += [(low, high), (high, low)]
        for end in (0, n - 1):
            pairs_b.append((end * levels + level, end * levels + (level + 1) % levels))
    far = lax.ppermute(pay, "lon", mirror)
    groups = (rows + 8) // 4
    pairs = (rows + 4) // 2
    sec_shape = shape((pairs * LINE, 256), BF)
    f_shape = shape((2, 2 * groups, 64, 256), BF)
    packed = (4, 5, 16, w1.shape[3])
    field = scratch((2, rows + 16, cols), F32)
    fold = scratch((2, 16, cols), F32)
    sec, w1_wide, f = call(
        south_body,
        [own, w1, b1, w2, b2],
        [sec_shape, shape(packed, BF), f_shape],
        [field, scratch((1, 3, 64 * SPLIT + 8, 256), F32)]
        + [scratch((5, 2, 8, w1.shape[3]), F32)]
        + [scratch(w2.shape, BF), sems(())],
        flops=2 * 64 * SPLIT * 256 * 4608,
        far_ins=(3,),
    )
    (both,) = call(pair_body, [pay, far], [shape((16, cols), BF)], [])
    near_a = lax.ppermute(both, "lon", pairs_a)
    near_b = lax.ppermute(both, ("lon", "lev"), pairs_b)
    sec, w3_wide, w4_wide, sel, _ = call(
        functools.partial(north_body, lon_count=n),
        [fold_pivot, own, far, w1_wide, b1, w2, b2, w3, w4, sec, f],
        [sec_shape, shape((256, 512), BF), shape((16, 512), BF), shape((256, 256), BF), f_shape],
        [field, fold, scratch((1, 3, 64 * (pairs - SPLIT) + 8, 256), F32)],
        flops=2 * 64 * (pairs - SPLIT) * 256 * 4608,
        aliases={9: 0, 10: 4},
    )
    out, _ = call(
        functools.partial(last_body, lon_count=n),
        [fold_pivot, lon, b4, vel, land, own, pay, far, near_a, near_b]
        + [w1_wide, b1, w2, b2, w3_wide, b3, w4_wide, sel, sec],
        [shape((2, rows, cols), BF), sec_shape],
        [
            field,
            fold,
            scratch((2, 2 * groups, 2 * EDGE, 256), BF),
            scratch((3, 2 * pairs * EDGE + 8, 256), F32),
            scratch((2, 2, pairs // 2 * LINE + 16, 128), F32),
            scratch((2, pairs * LINE, 128), BF),
            scratch((2, 64, 128), F32),
            scratch((2, rows, cols), F32),
        ],
        flops=2 * 64 * pairs * 256 * 1024,
        aliases={18: 1},
    )
    return out.reshape(velocity.shape)


def solution(mesh):
    in_specs = (
        P(None, ("members", "lev"), None, "lon"),
        P(("members", "lev"), None, "lon"),
    ) + (P(),) * 9
    out_specs = P(None, ("members", "lev"), None, "lon")
    return jax.shard_map(step, mesh=mesh, in_specs=in_specs, out_specs=out_specs, check_vma=False)
```

```python
import functools

import jax
import jax.numpy as jnp
from jax import lax
from jax.experimental import pallas as pl
from jax.experimental.pallas import tpu as pltpu
from jax.sharding import PartitionSpec as P

BF = jnp.bfloat16
F32 = jnp.float32
EDGE = 8
LINE = 80
SPLIT = 10


def dot(a, b):
    return jnp.dot(a, b, preferred_element_type=F32)


def dot_nt(a, b):
    return lax.dot_general(a, b, (((1,), (1,)), ((), ())), preferred_element_type=F32)


def iota(shape, dim):
    return lax.broadcasted_iota(jnp.int32, shape, dim)


def roll_lanes(x, shift):
    return pltpu.roll(x, shift % x.shape[1], axis=1)


def first_weights(w1_ref, row):
    zero = jnp.zeros(w1_ref.shape[2:], BF)
    sides = []
    for b in range(2):
        tiles = [w1_ref[row, t - b] if 0 <= t - b < 5 else zero for t in range(6)]
        sides.append(jnp.concatenate(tiles, axis=0))
    return jnp.concatenate(sides, axis=1)


def load_field(field_ref, values):
    rows = values[0].shape[0]
    for c in range(2):
        field_ref[c, 0:8, :] = jnp.zeros((8, values[0].shape[1]), F32)
        field_ref[c, rows : rows + 16, :] = jnp.zeros((16, values[0].shape[1]), F32)
        field_ref[c, 6 : rows + 6, :] = values[c]


def load_fold(fold_ref, tails):
    for c in range(2):
        fold_ref[c] = jnp.zeros(fold_ref.shape[1:], F32)
        for k in range(1, 7):
            fold_ref[c, 5 + k : 6 + k, :] = -tails[c][7 - k : 8 - k]


def patches(ref, start, shifted):
    tiles = []
    windows = [ref[c, start : start + 8, :] for c in range(2)]
    for t in range(6):
        tiles.append(jnp.concatenate([shifted(windows[c], t, c) for c in range(2)], axis=0))
    return jnp.concatenate(tiles, axis=0).astype(BF)


def left_sides(field_ref, fold_ref, pivot_ref, wide, pick, pick_fold, groups, rows):
    out = []
    for g in groups:
        part = dot_nt(pick, patches(field_ref, 4 * g, lambda x, t, c: roll_lanes(x, -t)))
        if 4 * g + 8 > rows + 6:
            ups = [
                jnp.broadcast_to(pivot_ref[:, c : c + 1], (8, pick.shape[1])) > wide - 1
                for c in range(2)
            ]

            def turned(x, t, c):
                return jnp.where(ups[c], roll_lanes(x, t - 1), roll_lanes(x, t + 1))

            part = part + dot_nt(pick_fold, patches(fold_ref, 4 * g - rows, turned))
        out.append(part)
    return out


def second_weights(w2_ref):
    zero = jnp.zeros(w2_ref.shape[2:], BF)
    rows = []
    for shift in range(3):
        for dr in range(2):
            for dc in range(2):
                cells = []
                for a in range(6):
                    for b in (2 * shift - dc, 2 * shift + 1 - dc):
                        inside = 0 <= a - dr < 5 and 0 <= b < 5
                        cells.append(w2_ref[a - dr, b] if inside else zero)
                rows.append(jnp.concatenate(cells, axis=1))
    return jnp.concatenate(rows, axis=0)


def block_weights(w_ref, shifts):
    zero = jnp.zeros(w_ref.shape[2:], F32)
    rows = []
    for dr in range(2):
        for dc in range(2):
            cells = []
            for er in range(2):
                for ec in shifts:
                    for r in range(2):
                        for c in range(2):
                            a, b = 2 * er + r - dr, 2 * ec + c - dc
                            inside = 0 <= a < 3 and 0 <= b < 3
                            cells.append(w_ref[a, b].astype(F32) if inside else zero)
            rows.append(jnp.concatenate(cells, axis=1))
    return rows


def edge_tile(values, blocks):
    lane = iota(values[0].shape, 1) >> 4
    tile = jnp.zeros(values[0].shape, F32)
    for value, block in zip(values, blocks):
        tile = jnp.where(lane == block, roll_lanes(value, 8 + 16 * block), tile)
    return tile


def mask_body(*refs, small):
    vel_hbm, land_hbm = refs[:2]
    own_ref, pay_ref = refs[2 + small : 4 + small]
    vel_ref, land_ref, sems = refs[4 + 2 * small :]
    moves = [(vel_hbm, vel_ref), (land_hbm, land_ref)]
    moves += list(zip(refs[2 : 2 + small], refs[4 + small : 4 + 2 * small]))
    copies = [pltpu.make_async_copy(a, b, sems.at[k]) for k, (a, b) in enumerate(moves)]
    for copy in copies:
        copy.start()
    for copy in copies[:2]:
        copy.wait()
    land = land_ref[...].astype(F32)
    own = [vel_ref[c].astype(F32) * land for c in range(2)]
    for c in range(2):
        own_ref[c] = own[c].astype(BF)
    rows = land.shape[0]
    tiles = [own[c][rows - 8 :] for c in range(2)]
    cuts = [own[c][k : k + 8] for c in range(2) for k in range(0, rows, 8)]
    tiles.append(edge_tile(cuts, range(len(cuts))))
    pay_ref[...] = jnp.concatenate(tiles, axis=0).astype(BF)
    for copy in copies[2:]:
        copy.wait()


def pair_body(pay_ref, far_ref, both_ref):
    far = far_ref[...].astype(F32)
    half = far.shape[1] // 32
    tile = edge_tile([far[0:8], far[8:16]], (half - 1, 2 * half - 1))
    own = pay_ref[...].astype(F32)[16:24]
    both_ref[...] = jnp.concatenate([own, tile], axis=0).astype(BF)


def pack_first(w1_ref, wide_ref, w1_out):
    wide_ref[...] = jnp.zeros_like(wide_ref)
    for t in range(5):
        for a in range(5):
            value = w1_ref[a, t].astype(F32)
            for c in range(2):
                wide_ref[t, c, a : a + 1, :] = value[c : c + 1]
    for t in range(5):
        base = [wide_ref[t, c] for c in range(2)]
        for row in range(4):
            both = [pltpu.roll(x, row, axis=0) if row else x for x in base]
            w1_out[row, t] = jnp.concatenate(both, axis=0).astype(BF)


def first_layer(lefts, f_ref, w1_ref, bias, start=0):
    stacked = jnp.concatenate(lefts, axis=0).astype(BF)
    size = lefts[0].shape[0]
    for row in range(4):
        res = dot(stacked, first_weights(w1_ref, row))
        res = jnp.maximum(res + bias, 0.0).astype(BF)
        for g in range(len(lefts)):
            f_ref[row % 2, 2 * (start + g) + row // 2] = res[size * g : size * g + size]


def second_layer(f_ref, right, acc_ref, lo, count):
    size = f_ref.shape[2]
    left = jnp.concatenate(
        [
            f_ref[a % 2, lo + a // 2 : lo + a // 2 + count].reshape(count * size, 256)
            for a in range(6)
        ],
        axis=1,
    )
    res = dot_nt(left, right)
    for shift in range(3):
        acc_ref[shift, 0 : count * size, :] = res[:, 256 * shift : 256 * shift + 256]


def shifted_sum(acc_ref, at, size, bias):
    parts = [acc_ref[k, at + k : at + k + size, :] for k in range(acc_ref.shape[0])]
    total = parts[0]
    for part in parts[1:]:
        total = total + part
    return jnp.maximum(total + bias, 0.0)


def inner_second(f_ref, right, bias, acc_ref, sec_ref, start, count):
    chunks = acc_ref.shape[0]
    step = count // chunks
    for k in range(chunks):
        second_layer(f_ref, right, acc_ref.at[k], start + k * step, step)
        for p in range(step):
            at = (start + k * step + p) * LINE
            sec_ref[at : at + 64, :] = shifted_sum(acc_ref.at[k], 64 * p, 64, bias).astype(BF)


def inner_picks(cols):
    lane = iota((64, cols), 1)
    slot = iota((64, cols), 0)
    fold = lax.rem(2 * cols + 5 - 2 * slot, cols)
    return (lane == 2 * slot - 6).astype(BF), (lane == fold).astype(BF)


def local_first(own_ref, w1_ref, b1_ref, w2_hbm, f, w1_out, w2_out, field, wide, sem):
    copy = pltpu.make_async_copy(w2_hbm, w2_out, sem)
    copy.start()
    pack_first(w1_ref, wide, w1_out)
    rows = own_ref.shape[1]
    cols = own_ref.shape[2]
    load_field(field, [own_ref[c].astype(F32) for c in range(2)])
    pick, _ = inner_picks(cols)
    lefts = left_sides(field, None, None, 0, pick, None, range((rows - 2) // 4 + 1), rows)
    first_layer(lefts, f, w1_out, jnp.concatenate([b1_ref[...]] * 2, axis=1))
    copy.wait()


def early_body(own_ref, w1_ref, b1_ref, w2_hbm, pay_in, pay, f, w1_out, w2_out, field, wide, sem):
    @pl.when(lax.axis_index("lon") == 0)
    def _():
        local_first(own_ref, w1_ref, b1_ref, w2_hbm, f, w1_out, w2_out, field, wide, sem)


def south_body(
    own_ref, w1_ref, b1_ref, w2_hbm, b2_ref, f_in, w1_in, w2_in, sec, f, w1_out, w2_out,
    field, acc, wide, sem,
):
    @pl.when(lax.axis_index("lon") != 0)
    def _():
        local_first(own_ref, w1_ref, b1_ref, w2_hbm, f, w1_out, w2_out, field, wide, sem)

    bias2 = jnp.concatenate([b2_ref[...]] * 4, axis=1)
    inner_second(f, second_weights(w2_out), bias2, acc, sec, 0, SPLIT)


def north_body(
    pivot_ref, own_ref, far_ref, w1_ref, b1_ref, w2_ref, b2_ref, w3_ref, w4_ref, sec_in,
    f_in, sec, w3_out, w4_out, sel_out, f, field, fold, acc, *, lon_count,
):
    bias1 = jnp.concatenate([b1_ref[...]] * 2, axis=1)
    bias2 = jnp.concatenate([b2_ref[...]] * 4, axis=1)
    rows = own_ref.shape[1]
    cols = own_ref.shape[2]
    blocks = block_weights(w3_ref, (0,)) + block_weights(w3_ref, (1,))
    w3_out[...] = jnp.concatenate(blocks, axis=0).astype(BF)
    tiny = block_weights(w4_ref, (0, 1))
    blank = jnp.zeros((4, tiny[0].shape[1]), F32)
    order = [tiny[0], tiny[2], blank, tiny[1], tiny[3], blank]
    w4_out[...] = jnp.concatenate(order, axis=0).astype(BF)
    src = iota((256, 256), 0)
    want = 2 * (src & 127) + (src >> 7)
    sel_out[...] = (iota((256, 256), 1) == want).astype(BF)
    load_field(field, [own_ref[c].astype(F32) for c in range(2)])
    far = far_ref[...].astype(F32)
    load_fold(fold, [far[8 * c : 8 * c + 8] for c in range(2)])
    pick, pick_fold = inner_picks(cols)
    groups = range((rows - 2) // 4 + 1, (rows + 8) // 4)
    lefts = left_sides(field, fold, pivot_ref, lon_count * cols, pick, pick_fold, groups, rows)
    first_layer(lefts, f, w1_ref, bias1, groups[0])
    count = (rows + 4) // 2 - SPLIT
    inner_second(f, second_weights(w2_ref), bias2, acc, sec, SPLIT, count)


def last_body(
    pivot_ref, lon_ref, b4_ref, vel_ref, land_ref, own_ref, pay_ref, far_ref, near_a_ref, near_b_ref,
    w1_ref, b1_ref, w2_ref, b2_ref, w3_ref, b3_ref, w4_ref, sel_ref, sec_in,
    out_ref, sec, field, fold, f, acc, acc3, third, spill, tend, *, lon_count,
):
    rows = own_ref.shape[1]
    cols = own_ref.shape[2]
    bias1 = jnp.concatenate([b1_ref[...]] * 2, axis=1)
    bias2 = jnp.concatenate([b2_ref[...]] * 4, axis=1)
    bias3 = jnp.concatenate([b3_ref[...]] * 4, axis=1)
    groups = (rows + 8) // 4
    pairs = (rows + 4) // 2

    lon = jnp.broadcast_to(lon_ref[...], (16, cols))
    even = (lon & 1) == 0
    own = own_ref[...].astype(F32)
    far = far_ref[...].astype(F32)
    wrap = jnp.concatenate([far[16:24], pay_ref[...].astype(F32)[16:24]], axis=0)
    near_a = near_a_ref[...].astype(F32)
    near_b = near_b_ref[...].astype(F32)
    west = jnp.where(lon == 0, wrap, jnp.where(even, near_b, near_a))
    east = jnp.where(lon == lon_count - 1, wrap, jnp.where(even, near_a, near_b))
    lane = iota((8, cols), 1)
    half = cols // 2

    def around(mid, after, before, block):
        outer = jnp.where(
            lane < half // 2,
            roll_lanes(after, -16 * block - 8),
            roll_lanes(before, half - 8 - 16 * block),
        )
        inner = jnp.where(lane < half + half // 2, roll_lanes(mid, half), mid)
        return jnp.where(lane < half, outer, inner)

    wide = []
    tails = []
    for c in range(2):
        parts = []
        for k in range(rows // 8):
            block = c * (rows // 8) + k
            parts.append(around(own[c, 8 * k : 8 * k + 8], east[0:8], west[0:8], block))
        wide.append(jnp.concatenate(parts, axis=0))
        tails.append(around(far[8 * c : 8 * c + 8], west[8:16], east[8:16], block))
    load_field(field, wide)
    load_fold(fold, tails)
    slot = iota((2 * EDGE, cols), 0)
    lane = iota((2 * EDGE, cols), 1)
    low = slot < EDGE
    pair = jnp.where(low, slot, slot + (cols // 2 - 2 - EDGE))
    start = 2 * pair - 6 + jnp.where(low, cols // 2, 0)
    pick = (lane == lax.rem(start + cols, cols)).astype(BF)
    start = cols + 5 - 2 * pair + jnp.where(low, 0, cols // 2)
    pick_fold = (lane == lax.rem(start + cols, cols)).astype(BF)
    lefts = left_sides(
        field, fold, pivot_ref, lon_count * cols, pick, pick_fold, range(groups), rows
    )
    first_layer(lefts, f, w1_ref, bias1)
    second_layer(f, second_weights(w2_ref), acc, 0, pairs)
    line = iota((2 * EDGE, 256), 0)
    for k in range(pairs):
        at = k * LINE
        new = shifted_sum(acc, 2 * EDGE * k, 2 * EDGE, bias2)
        old = sec_in[at : at + 16, :].astype(F32)
        sec[at : at + 16, :] = jnp.where(line < 4, new, old).astype(BF)
        new = pltpu.roll(new, 6, axis=0)
        old = sec_in[at + 48 : at + 64, :].astype(F32)
        sec[at + 48 : at + 64, :] = jnp.where(line >= 14, new, old).astype(BF)
        sec[at + 64 : at + 80, :] = new.astype(BF)

    pairs3 = pairs - 1
    right = w3_ref[...]
    middle = (pairs3 + 1) // 2
    for part, (lo, hi) in enumerate(((0, middle), (middle, pairs3))):
        base, size = lo * LINE, (hi - lo) * LINE
        left = [sec[base + at : base + at + size, :] for at in (0, LINE)]
        res = dot_nt(jnp.concatenate(left, axis=1), right)
        for shift in range(2):
            acc3[part, shift, 0:size, :] = res[:, 128 * shift : 128 * shift + 128]
        for shift in range(2):
            value = shifted_sum(acc3.at[part], shift, size, bias3)
            third[shift, base : base + size, :] = value.astype(BF)

    pairs4 = pairs - 2
    right = w4_ref[...]
    tiles = []
    for lo in (0, pairs4 // 2):
        left = jnp.concatenate(
            [
                jnp.concatenate(
                    [
                        third[shift, k * LINE : k * LINE + 64, :]
                        for k in range(lo + up, lo + up + pairs4 // 2)
                    ],
                    axis=0,
                )
                for up in range(2)
                for shift in range(2)
            ],
            axis=1,
        )
        res = dot_nt(right, left)
        tiles += [res[:, 128 * t : 128 * t + 128] for t in range(pairs4 // 4)]
    stack = jnp.concatenate(
        [jnp.concatenate([x[8 * dc : 8 * dc + 8] for x in tiles], axis=0) for dc in range(2)], axis=1
    )
    upper = stack.astype(BF)
    lower = (stack - upper.astype(F32)).astype(BF)
    res = dot(jnp.concatenate([upper, lower], axis=0), sel_ref[...])
    count = 8 * len(tiles)
    res = res[:count] + res[count:]
    for k in range(2):
        spill[k] = res[:, 128 * k : 128 * k + 128]
    for c in range(2):
        for dr in range(2):
            for k in range(2):
                tend[c, pl.ds(2 * k + dr, pairs4 // 2, stride=4), :] = spill[
                    k, pl.ds(dr * 2 + c, pairs4 // 2, stride=8), :
                ]
    land = land_ref[...].astype(F32)
    for c in range(2):
        bias4 = jnp.broadcast_to(b4_ref[:, c : c + 1], (1, cols))
        total = vel_ref[c].astype(F32) + (tend[c] + bias4)
        out_ref[c] = (land * total).astype(BF)


def call(fn, ins, outs, scratch, flops=0, aliases=None, far_ins=()):
    vmem = pl.BlockSpec(memory_space=pltpu.VMEM)
    hbm = pl.BlockSpec(memory_space=pltpu.HBM)
    specs = [vmem] * len(ins)
    ins = list(ins)
    for k in far_ins:
        specs[k] = hbm
        ins[k] = pltpu.with_memory_space_constraint(ins[k], pltpu.HBM)
    return pl.pallas_call(
        fn,
        out_shape=outs,
        in_specs=specs,
        out_specs=[vmem] * len(outs),
        scratch_shapes=scratch,
        input_output_aliases=aliases or {},
        cost_estimate=pl.CostEstimate(flops=flops, bytes_accessed=1 << 20, transcendentals=0),
        compiler_params=pltpu.CompilerParams(
            vmem_limit_bytes=32 << 20
        ),
    )(*ins)


def step(velocity, land_sea, fold_pivot, w1, b1, w2, b2, w3, b3, w4, b4):
    rows = velocity.shape[2]
    cols = velocity.shape[3]
    n = lax.axis_size("lon")
    lon = jnp.full((1, 1), lax.axis_index("lon"), jnp.int32)
    vel = velocity.reshape(2, rows, cols)
    land = land_sea.reshape(rows, cols)
    w2, w3, w4 = (jnp.swapaxes(w, 2, 3) for w in (w2, w3, w4))
    b1, b2, b3, b4, fold_pivot = (x[None] for x in (b1, b2, b3, b4, fold_pivot))
    shape = jax.ShapeDtypeStruct
    scratch = pltpu.VMEM
    sems = pltpu.SemaphoreType.DMA
    near = [w1, b1, b2, b3, b4, fold_pivot]
    own, pay, w1, b1, b2, b3, b4, fold_pivot = call(
        functools.partial(mask_body, small=len(near)),
        [vel, land] + near,
        [shape(vel.shape, BF), shape((24, cols), BF)] + [shape(x.shape, x.dtype) for x in near],
        [scratch(vel.shape, BF), scratch(land.shape, jnp.int32), sems((2 + len(near),))],
        far_ins=range(2 + len(near)),
    )
    mirror = [(i, n - 1 - i) for i in range(n)]
    pairs_a = [(i, i ^ 1) for i in range(n)]
    levels = lax.axis_size("lev")
    pairs_b = []
    for level in range(levels):
        for k in range(1, n // 2):
            low, high = (2 * k - 1) * levels + level, 2 * k * levels + level
            pairs_b += [(low, high), (high, low)]
        for end in (0, n - 1):
            pairs_b.append((end * levels + level, end * levels + (level + 1) % levels))
    groups = (rows + 8) // 4
    pairs = (rows + 4) // 2
    sec_shape = shape((pairs * LINE, 256), BF)
    f_shape = shape((2, 2 * groups, 64, 256), BF)
    packed = (4, 5, 16, w1.shape[3])
    field = scratch((2, rows + 16, cols), F32)
    fold = scratch((2, 16, cols), F32)
    made = [f_shape, shape(packed, BF), shape(w2.shape, BF)]
    wide = scratch((5, 2, 8, w1.shape[3]), F32)
    pay, f, w1_wide, w2_near = call(
        early_body,
        [own, w1, b1, w2, pay],
        [shape(pay.shape, BF)] + made,
        [field, wide, sems(())],
        far_ins=(3,),
        aliases={4: 0},
    )
    far = lax.ppermute(pay, "lon", mirror)
    sec, f, w1_wide, w2 = call(
        south_body,
        [own, w1, b1, w2, b2, f, w1_wide, w2_near],
        [sec_shape] + made,
        [field, scratch((1, 3, 64 * SPLIT + 8, 256), F32), wide, sems(())],
        flops=2 * 64 * SPLIT * 256 * 4608,
        far_ins=(3,),
        aliases={5: 1, 6: 2, 7: 3},
    )
    (both,) = call(pair_body, [pay, far], [shape((16, cols), BF)], [])
    near_a = lax.ppermute(both, "lon", pairs_a)
    near_b = lax.ppermute(both, ("lon", "lev"), pairs_b)
    sec, w3_wide, w4_wide, sel, _ = call(
        functools.partial(north_body, lon_count=n),
        [fold_pivot, own, far, w1_wide, b1, w2, b2, w3, w4, sec, f],
        [sec_shape, shape((256, 512), BF), shape((16, 512), BF), shape((256, 256), BF), f_shape],
        [field, fold, scratch((1, 3, 64 * (pairs - SPLIT) + 8, 256), F32)],
        flops=2 * 64 * (pairs - SPLIT) * 256 * 4608,
        aliases={9: 0, 10: 4},
    )
    out, _ = call(
        functools.partial(last_body, lon_count=n),
        [fold_pivot, lon, b4, vel, land, own, pay, far, near_a, near_b]
        + [w1_wide, b1, w2, b2, w3_wide, b3, w4_wide, sel, sec],
        [shape((2, rows, cols), BF), sec_shape],
        [
            field,
            fold,
            scratch((2, 2 * groups, 2 * EDGE, 256), BF),
            scratch((3, 2 * pairs * EDGE + 8, 256), F32),
            scratch((2, 2, pairs // 2 * LINE + 16, 128), F32),
            scratch((2, pairs * LINE, 128), BF),
            scratch((2, 64, 128), F32),
            scratch((2, rows, cols), F32),
        ],
        flops=2 * 64 * pairs * 256 * 1024,
        aliases={18: 1},
    )
    return out.reshape(velocity.shape)


def solution(mesh):
    in_specs = (
        P(None, ("members", "lev"), None, "lon"),
        P(("members", "lev"), None, "lon"),
    ) + (P(),) * 9
    out_specs = P(None, ("members", "lev"), None, "lon")
    return jax.shard_map(step, mesh=mesh, in_specs=in_specs, out_specs=out_specs, check_vma=False)
```

```python
import functools

import jax
import jax.numpy as jnp
from jax import lax
from jax.experimental import pallas as pl
from jax.experimental.pallas import tpu as pltpu
from jax.sharding import PartitionSpec as P

BF = jnp.bfloat16
F32 = jnp.float32
EDGE = 8
LINE = 80
SPLIT = 10


def dot(a, b):
    return jnp.dot(a, b, preferred_element_type=F32)


def dot_nt(a, b):
    return lax.dot_general(a, b, (((1,), (1,)), ((), ())), preferred_element_type=F32)


def iota(shape, dim):
    return lax.broadcasted_iota(jnp.int32, shape, dim)


def roll_lanes(x, shift):
    return pltpu.roll(x, shift % x.shape[1], axis=1)


def first_weights(w1_ref, row):
    zero = jnp.zeros(w1_ref.shape[2:], BF)
    sides = []
    for b in range(2):
        tiles = [w1_ref[row, t - b] if 0 <= t - b < 5 else zero for t in range(6)]
        sides.append(jnp.concatenate(tiles, axis=0))
    return jnp.concatenate(sides, axis=1)


def load_field(field_ref, values):
    rows = values[0].shape[0]
    for c in range(2):
        field_ref[c, 0:8, :] = jnp.zeros((8, values[0].shape[1]), F32)
        field_ref[c, rows : rows + 16, :] = jnp.zeros((16, values[0].shape[1]), F32)
        field_ref[c, 6 : rows + 6, :] = values[c]


def load_fold(fold_ref, tails):
    for c in range(2):
        fold_ref[c] = jnp.zeros(fold_ref.shape[1:], F32)
        for k in range(1, 7):
            fold_ref[c, 5 + k : 6 + k, :] = -tails[c][7 - k : 8 - k]


def patches(ref, start, shifted):
    tiles = []
    windows = [ref[c, start : start + 8, :] for c in range(2)]
    for t in range(6):
        tiles.append(jnp.concatenate([shifted(windows[c], t, c) for c in range(2)], axis=0))
    return jnp.concatenate(tiles, axis=0).astype(BF)


def left_sides(field_ref, fold_ref, pivot_ref, wide, pick, pick_fold, groups, rows):
    out = []
    for g in groups:
        part = dot_nt(pick, patches(field_ref, 4 * g, lambda x, t, c: roll_lanes(x, -t)))
        if 4 * g + 8 > rows + 6:
            ups = [
                jnp.broadcast_to(pivot_ref[:, c : c + 1], (8, pick.shape[1])) > wide - 1
                for c in range(2)
            ]

            def turned(x, t, c):
                return jnp.where(ups[c], roll_lanes(x, t - 1), roll_lanes(x, t + 1))

            part = part + dot_nt(pick_fold, patches(fold_ref, 4 * g - rows, turned))
        out.append(part)
    return out


def second_weights(w2_ref):
    zero = jnp.zeros(w2_ref.shape[2:], BF)
    rows = []
    for shift in range(3):
        for dr in range(2):
            for dc in range(2):
                cells = []
                for a in range(6):
                    for b in (2 * shift - dc, 2 * shift + 1 - dc):
                        inside = 0 <= a - dr < 5 and 0 <= b < 5
                        cells.append(w2_ref[a - dr, b] if inside else zero)
                rows.append(jnp.concatenate(cells, axis=1))
    return jnp.concatenate(rows, axis=0)


def block_weights(w_ref, shifts):
    zero = jnp.zeros(w_ref.shape[2:], F32)
    rows = []
    for dr in range(2):
        for dc in range(2):
            cells = []
            for er in range(2):
                for ec in shifts:
                    for r in range(2):
                        for c in range(2):
                            a, b = 2 * er + r - dr, 2 * ec + c - dc
                            inside = 0 <= a < 3 and 0 <= b < 3
                            cells.append(w_ref[a, b].astype(F32) if inside else zero)
            rows.append(jnp.concatenate(cells, axis=1))
    return rows


def edge_tile(values, blocks):
    lane = iota(values[0].shape, 1) >> 4
    tile = jnp.zeros(values[0].shape, F32)
    for value, block in zip(values, blocks):
        tile = jnp.where(lane == block, roll_lanes(value, 8 + 16 * block), tile)
    return tile


def mask_body(*refs, small):
    vel_hbm, land_hbm = refs[:2]
    own_ref, pay_ref = refs[2 + small : 4 + small]
    vel_ref, land_ref, sems = refs[4 + 2 * small :]
    moves = [(vel_hbm, vel_ref), (land_hbm, land_ref)]
    moves += list(zip(refs[2 : 2 + small], refs[4 + small : 4 + 2 * small]))
    copies = [pltpu.make_async_copy(a, b, sems.at[k]) for k, (a, b) in enumerate(moves)]
    for copy in copies:
        copy.start()
    for copy in copies[:2]:
        copy.wait()
    land = land_ref[...].astype(F32)
    own = [vel_ref[c].astype(F32) * land for c in range(2)]
    for c in range(2):
        own_ref[c] = own[c].astype(BF)
    rows = land.shape[0]
    tiles = [own[c][rows - 8 :] for c in range(2)]
    cuts = [own[c][k : k + 8] for c in range(2) for k in range(0, rows, 8)]
    tiles.append(edge_tile(cuts, range(len(cuts))))
    pay_ref[...] = jnp.concatenate(tiles, axis=0).astype(BF)
    for copy in copies[2:]:
        copy.wait()


def pair_body(pay_ref, far_ref, both_ref):
    far = far_ref[...].astype(F32)
    half = far.shape[1] // 32
    tile = edge_tile([far[0:8], far[8:16]], (half - 1, 2 * half - 1))
    own = pay_ref[...].astype(F32)[16:24]
    both_ref[...] = jnp.concatenate([own, tile], axis=0).astype(BF)


def pack_first(w1_ref, wide_ref, w1_out):
    wide_ref[...] = jnp.zeros_like(wide_ref)
    for t in range(5):
        for a in range(5):
            value = w1_ref[a, t].astype(F32)
            for c in range(2):
                wide_ref[t, c, a : a + 1, :] = value[c : c + 1]
    for t in range(5):
        base = [wide_ref[t, c] for c in range(2)]
        for row in range(4):
            both = [pltpu.roll(x, row, axis=0) if row else x for x in base]
            w1_out[row, t] = jnp.concatenate(both, axis=0).astype(BF)


def first_layer(lefts, f_ref, w1_ref, bias, start=0):
    stacked = jnp.concatenate(lefts, axis=0).astype(BF)
    size = lefts[0].shape[0]
    for row in range(4):
        res = dot(stacked, first_weights(w1_ref, row))
        res = jnp.maximum(res + bias, 0.0).astype(BF)
        for g in range(len(lefts)):
            f_ref[row % 2, 2 * (start + g) + row // 2] = res[size * g : size * g + size]


def second_layer(f_ref, right, acc_ref, lo, count):
    size = f_ref.shape[2]
    left = jnp.concatenate(
        [
            f_ref[a % 2, lo + a // 2 : lo + a // 2 + count].reshape(count * size, 256)
            for a in range(6)
        ],
        axis=1,
    )
    res = dot_nt(left, right)
    for shift in range(3):
        acc_ref[shift, 0 : count * size, :] = res[:, 256 * shift : 256 * shift + 256]


def shifted_sum(acc_ref, at, size, bias):
    parts = [acc_ref[k, at + k : at + k + size, :] for k in range(acc_ref.shape[0])]
    total = parts[0]
    for part in parts[1:]:
        total = total + part
    return jnp.maximum(total + bias, 0.0)


def inner_second(f_ref, right, bias, acc_ref, sec_ref, start, count):
    chunks = acc_ref.shape[0]
    step = count // chunks
    for k in range(chunks):
        second_layer(f_ref, right, acc_ref.at[k], start + k * step, step)
        for p in range(step):
            at = (start + k * step + p) * LINE
            sec_ref[at : at + 64, :] = shifted_sum(acc_ref.at[k], 64 * p, 64, bias).astype(BF)


def inner_picks(cols):
    lane = iota((64, cols), 1)
    slot = iota((64, cols), 0)
    fold = lax.rem(2 * cols + 5 - 2 * slot, cols)
    return (lane == 2 * slot - 6).astype(BF), (lane == fold).astype(BF)


def local_first(own_ref, w1_ref, b1_ref, w2_hbm, f, w1_out, w2_out, field, wide, sem):
    copy = pltpu.make_async_copy(w2_hbm, w2_out, sem)
    copy.start()
    pack_first(w1_ref, wide, w1_out)
    rows = own_ref.shape[1]
    cols = own_ref.shape[2]
    load_field(field, [own_ref[c].astype(F32) for c in range(2)])
    pick, _ = inner_picks(cols)
    lefts = left_sides(field, None, None, 0, pick, None, range((rows - 2) // 4 + 1), rows)
    first_layer(lefts, f, w1_out, jnp.concatenate([b1_ref[...]] * 2, axis=1))
    copy.wait()


def early_body(own_ref, w1_ref, b1_ref, w2_hbm, pay_in, pay, f, w1_out, w2_out, field, wide, sem):
    @pl.when(lax.axis_index("lon") == 0)
    def _():
        local_first(own_ref, w1_ref, b1_ref, w2_hbm, f, w1_out, w2_out, field, wide, sem)


def south_body(
    own_ref, w1_ref, b1_ref, w2_hbm, b2_ref, f_in, w1_in, w2_in, sec, f, w1_out, w2_out,
    field, acc, wide, sem,
):
    @pl.when(lax.axis_index("lon") != 0)
    def _():
        local_first(own_ref, w1_ref, b1_ref, w2_hbm, f, w1_out, w2_out, field, wide, sem)

    bias2 = jnp.concatenate([b2_ref[...]] * 4, axis=1)
    inner_second(f, second_weights(w2_out), bias2, acc, sec, 0, SPLIT)


def north_body(
    pivot_ref, own_ref, far_ref, w1_ref, b1_ref, w2_ref, b2_ref, w3_ref, w4_ref, sec_in,
    f_in, sec, w3_out, w4_out, sel_out, f, field, fold, acc, *, lon_count,
):
    bias1 = jnp.concatenate([b1_ref[...]] * 2, axis=1)
    bias2 = jnp.concatenate([b2_ref[...]] * 4, axis=1)
    rows = own_ref.shape[1]
    cols = own_ref.shape[2]
    blocks = block_weights(w3_ref, (0,)) + block_weights(w3_ref, (1,))
    w3_out[...] = jnp.concatenate(blocks, axis=0).astype(BF)
    tiny = block_weights(w4_ref, (0, 1))
    blank = jnp.zeros((4, tiny[0].shape[1]), F32)
    order = [tiny[0], tiny[2], blank, tiny[1], tiny[3], blank]
    w4_out[...] = jnp.concatenate(order, axis=0).astype(BF)
    src = iota((256, 256), 0)
    want = 2 * (src & 127) + (src >> 7)
    sel_out[...] = (iota((256, 256), 1) == want).astype(BF)
    load_field(field, [own_ref[c].astype(F32) for c in range(2)])
    far = far_ref[...].astype(F32)
    load_fold(fold, [far[8 * c : 8 * c + 8] for c in range(2)])
    pick, pick_fold = inner_picks(cols)
    groups = range((rows - 2) // 4 + 1, (rows + 8) // 4)
    lefts = left_sides(field, fold, pivot_ref, lon_count * cols, pick, pick_fold, groups, rows)
    first_layer(lefts, f, w1_ref, bias1, groups[0])
    count = (rows + 4) // 2 - SPLIT
    inner_second(f, second_weights(w2_ref), bias2, acc, sec, SPLIT, count)


def last_body(
    pivot_ref, lon_ref, b4_ref, vel_ref, land_ref, own_ref, pay_ref, far_ref, near_a_ref, near_b_ref,
    w1_ref, b1_ref, w2_ref, b2_ref, w3_ref, b3_ref, w4_ref, sel_ref, sec_in,
    out_ref, field, fold, f, acc, strip, accs, acc3, third, spill, tend, *, lon_count,
):
    rows = own_ref.shape[1]
    cols = own_ref.shape[2]
    bias1 = jnp.concatenate([b1_ref[...]] * 2, axis=1)
    bias2 = jnp.concatenate([b2_ref[...]] * 4, axis=1)
    bias3 = jnp.concatenate([b3_ref[...]] * 4, axis=1)
    groups = (rows + 8) // 4
    pairs = (rows + 4) // 2

    lon = jnp.broadcast_to(lon_ref[...], (16, cols))
    even = (lon & 1) == 0
    own = own_ref[...].astype(F32)
    far = far_ref[...].astype(F32)
    wrap = jnp.concatenate([far[16:24], pay_ref[...].astype(F32)[16:24]], axis=0)
    near_a = near_a_ref[...].astype(F32)
    near_b = near_b_ref[...].astype(F32)
    west = jnp.where(lon == 0, wrap, jnp.where(even, near_b, near_a))
    east = jnp.where(lon == lon_count - 1, wrap, jnp.where(even, near_a, near_b))
    lane = iota((8, cols), 1)
    half = cols // 2

    def around(mid, after, before, block):
        outer = jnp.where(
            lane < half // 2,
            roll_lanes(after, -16 * block - 8),
            roll_lanes(before, half - 8 - 16 * block),
        )
        inner = jnp.where(lane < half + half // 2, roll_lanes(mid, half), mid)
        return jnp.where(lane < half, outer, inner)

    wide = []
    tails = []
    for c in range(2):
        parts = []
        for k in range(rows // 8):
            block = c * (rows // 8) + k
            parts.append(around(own[c, 8 * k : 8 * k + 8], east[0:8], west[0:8], block))
        wide.append(jnp.concatenate(parts, axis=0))
        tails.append(around(far[8 * c : 8 * c + 8], west[8:16], east[8:16], block))
    load_field(field, wide)
    load_fold(fold, tails)
    slot = iota((2 * EDGE, cols), 0)
    lane = iota((2 * EDGE, cols), 1)
    low = slot < EDGE
    pair = jnp.where(low, slot, slot + (cols // 2 - 4 - EDGE))
    start = 2 * pair - 6 + jnp.where(low, cols // 2, 0)
    pick = (lane == lax.rem(start + cols, cols)).astype(BF)
    start = cols + 5 - 2 * pair + jnp.where(low, 0, cols // 2)
    pick_fold = (lane == lax.rem(start + cols, cols)).astype(BF)
    lefts = left_sides(
        field, fold, pivot_ref, lon_count * cols, pick, pick_fold, range(groups), rows
    )
    first_layer(lefts, f, w1_ref, bias1)
    second_layer(f, second_weights(w2_ref), acc, 0, pairs)
    pairs3 = pairs - 1
    right = w3_ref[...]
    middle = (pairs3 + 1) // 2
    for part, (lo, hi) in enumerate(((0, middle), (middle, pairs3))):
        base, size = lo * LINE, (hi - lo) * LINE
        left = [sec_in[base + at : base + at + size, :] for at in (0, LINE)]
        res = dot_nt(jnp.concatenate(left, axis=1), right)
        for shift in range(2):
            acc3[part, shift, 0:size, :] = res[:, 128 * shift : 128 * shift + 128]
        for shift in range(2):
            value = shifted_sum(acc3.at[part], shift, size, bias3)
            third[shift, base : base + size, :] = value.astype(BF)

    strip[...] = shifted_sum(acc, 0, 2 * EDGE * pairs, bias2).astype(BF)
    size = 2 * EDGE * pairs3
    res = dot_nt(jnp.concatenate([strip[0:size], strip[2 * EDGE :]], axis=1), w3_ref[...])
    for shift in range(2):
        accs[shift, 0:size, :] = res[:, 128 * shift : 128 * shift + 128]
    line = iota((2 * EDGE, 128), 0)
    for shift in range(2):
        edge = shifted_sum(accs, shift, size, bias3)
        for k in range(pairs3):
            new = edge[2 * EDGE * k : 2 * EDGE * k + 2 * EDGE]
            at = k * LINE
            old = third[shift, at : at + 16, :].astype(F32)
            third[shift, at : at + 16, :] = jnp.where(line < 4, new, old).astype(BF)
            at += 48
            new = pltpu.roll(new, 4, axis=0)
            old = third[shift, at : at + 16, :].astype(F32)
            third[shift, at : at + 16, :] = jnp.where(line >= 12, new, old).astype(BF)

    pairs4 = pairs - 2
    right = w4_ref[...]
    tiles = []
    for lo in (0, pairs4 // 2):
        left = jnp.concatenate(
            [
                jnp.concatenate(
                    [
                        third[shift, k * LINE : k * LINE + 64, :]
                        for k in range(lo + up, lo + up + pairs4 // 2)
                    ],
                    axis=0,
                )
                for up in range(2)
                for shift in range(2)
            ],
            axis=1,
        )
        res = dot_nt(right, left)
        tiles += [res[:, 128 * t : 128 * t + 128] for t in range(pairs4 // 4)]
    stack = jnp.concatenate(
        [jnp.concatenate([x[8 * dc : 8 * dc + 8] for x in tiles], axis=0) for dc in range(2)], axis=1
    )
    upper = stack.astype(BF)
    lower = (stack - upper.astype(F32)).astype(BF)
    res = dot(jnp.concatenate([upper, lower], axis=0), sel_ref[...])
    count = 8 * len(tiles)
    res = res[:count] + res[count:]
    for k in range(2):
        spill[k] = res[:, 128 * k : 128 * k + 128]
    for c in range(2):
        for dr in range(2):
            for k in range(2):
                tend[c, pl.ds(2 * k + dr, pairs4 // 2, stride=4), :] = spill[
                    k, pl.ds(dr * 2 + c, pairs4 // 2, stride=8), :
                ]
    land = land_ref[...].astype(F32)
    for c in range(2):
        bias4 = jnp.broadcast_to(b4_ref[:, c : c + 1], (1, cols))
        total = vel_ref[c].astype(F32) + (tend[c] + bias4)
        out_ref[c] = (land * total).astype(BF)


def call(fn, ins, outs, scratch, flops=0, aliases=None, far_ins=()):
    vmem = pl.BlockSpec(memory_space=pltpu.VMEM)
    hbm = pl.BlockSpec(memory_space=pltpu.HBM)
    specs = [vmem] * len(ins)
    ins = list(ins)
    for k in far_ins:
        specs[k] = hbm
        ins[k] = pltpu.with_memory_space_constraint(ins[k], pltpu.HBM)
    return pl.pallas_call(
        fn,
        out_shape=outs,
        in_specs=specs,
        out_specs=[vmem] * len(outs),
        scratch_shapes=scratch,
        input_output_aliases=aliases or {},
        cost_estimate=pl.CostEstimate(flops=flops, bytes_accessed=1 << 20, transcendentals=0),
        compiler_params=pltpu.CompilerParams(
            vmem_limit_bytes=32 << 20
        ),
    )(*ins)


def step(velocity, land_sea, fold_pivot, w1, b1, w2, b2, w3, b3, w4, b4):
    rows = velocity.shape[2]
    cols = velocity.shape[3]
    n = lax.axis_size("lon")
    lon = jnp.full((1, 1), lax.axis_index("lon"), jnp.int32)
    vel = velocity.reshape(2, rows, cols)
    land = land_sea.reshape(rows, cols)
    w2, w3, w4 = (jnp.swapaxes(w, 2, 3) for w in (w2, w3, w4))
    b1, b2, b3, b4, fold_pivot = (x[None] for x in (b1, b2, b3, b4, fold_pivot))
    shape = jax.ShapeDtypeStruct
    scratch = pltpu.VMEM
    sems = pltpu.SemaphoreType.DMA
    near = [w1, b1, b2, b3, b4, fold_pivot]
    own, pay, w1, b1, b2, b3, b4, fold_pivot = call(
        functools.partial(mask_body, small=len(near)),
        [vel, land] + near,
        [shape(vel.shape, BF), shape((24, cols), BF)] + [shape(x.shape, x.dtype) for x in near],
        [scratch(vel.shape, BF), scratch(land.shape, jnp.int32), sems((2 + len(near),))],
        far_ins=range(2 + len(near)),
    )
    mirror = [(i, n - 1 - i) for i in range(n)]
    pairs_a = [(i, i ^ 1) for i in range(n)]
    levels = lax.axis_size("lev")
    pairs_b = []
    for level in range(levels):
        for k in range(1, n // 2):
            low, high = (2 * k - 1) * levels + level, 2 * k * levels + level
            pairs_b += [(low, high), (high, low)]
        for end in (0, n - 1):
            pairs_b.append((end * levels + level, end * levels + (level + 1) % levels))
    groups = (rows + 8) // 4
    pairs = (rows + 4) // 2
    sec_shape = shape((pairs * LINE, 256), BF)
    f_shape = shape((2, 2 * groups, 64, 256), BF)
    packed = (4, 5, 16, w1.shape[3])
    field = scratch((2, rows + 16, cols), F32)
    fold = scratch((2, 16, cols), F32)
    made = [f_shape, shape(packed, BF), shape(w2.shape, BF)]
    wide = scratch((5, 2, 8, w1.shape[3]), F32)
    pay, f, w1_wide, w2_near = call(
        early_body,
        [own, w1, b1, w2, pay],
        [shape(pay.shape, BF)] + made,
        [field, wide, sems(())],
        far_ins=(3,),
        aliases={4: 0},
    )
    far = lax.ppermute(pay, "lon", mirror)
    sec, f, w1_wide, w2 = call(
        south_body,
        [own, w1, b1, w2, b2, f, w1_wide, w2_near],
        [sec_shape] + made,
        [field, scratch((1, 3, 64 * SPLIT + 8, 256), F32), wide, sems(())],
        flops=2 * 64 * SPLIT * 256 * 4608,
        far_ins=(3,),
        aliases={5: 1, 6: 2, 7: 3},
    )
    (both,) = call(pair_body, [pay, far], [shape((16, cols), BF)], [])
    near_a = lax.ppermute(both, "lon", pairs_a)
    near_b = lax.ppermute(both, ("lon", "lev"), pairs_b)
    sec, w3_wide, w4_wide, sel, _ = call(
        functools.partial(north_body, lon_count=n),
        [fold_pivot, own, far, w1_wide, b1, w2, b2, w3, w4, sec, f],
        [sec_shape, shape((256, 512), BF), shape((16, 512), BF), shape((256, 256), BF), f_shape],
        [field, fold, scratch((1, 3, 64 * (pairs - SPLIT) + 8, 256), F32)],
        flops=2 * 64 * (pairs - SPLIT) * 256 * 4608,
        aliases={9: 0, 10: 4},
    )
    (out,) = call(
        functools.partial(last_body, lon_count=n),
        [fold_pivot, lon, b4, vel, land, own, pay, far, near_a, near_b]
        + [w1_wide, b1, w2, b2, w3_wide, b3, w4_wide, sel, sec],
        [shape((2, rows, cols), BF)],
        [
            field,
            fold,
            scratch((2, 2 * groups, 2 * EDGE, 256), BF),
            scratch((3, 2 * pairs * EDGE + 8, 256), F32),
            scratch((2 * pairs * EDGE, 256), BF),
            scratch((2, 2 * pairs * EDGE + 8, 128), F32),
            scratch((2, 2, pairs // 2 * LINE + 16, 128), F32),
            scratch((2, pairs * LINE, 128), BF),
            scratch((2, 64, 128), F32),
            scratch((2, rows, cols), F32),
        ],
        flops=2 * 64 * pairs * 256 * 1024,
    )
    return out.reshape(velocity.shape)


def solution(mesh):
    in_specs = (
        P(None, ("members", "lev"), None, "lon"),
        P(("members", "lev"), None, "lon"),
    ) + (P(),) * 9
    out_specs = P(None, ("members", "lev"), None, "lon")
    return jax.shard_map(step, mesh=mesh, in_specs=in_specs, out_specs=out_specs, check_vma=False)
```

```python
import functools

import jax
import jax.numpy as jnp
from jax import lax
from jax.experimental import pallas as pl
from jax.experimental.pallas import tpu as pltpu
from jax.sharding import PartitionSpec as P

BF = jnp.bfloat16
F32 = jnp.float32
EDGE = 8
LINE = 80
SPLIT = 10


def dot(a, b):
    return jnp.dot(a, b, preferred_element_type=F32)


def dot_nt(a, b):
    return lax.dot_general(a, b, (((1,), (1,)), ((), ())), preferred_element_type=F32)


def iota(shape, dim):
    return lax.broadcasted_iota(jnp.int32, shape, dim)


def roll_lanes(x, shift):
    return pltpu.roll(x, shift % x.shape[1], axis=1)


def first_weights(w1_ref, row):
    zero = jnp.zeros(w1_ref.shape[2:], BF)
    sides = []
    for b in range(2):
        tiles = [w1_ref[row, t - b] if 0 <= t - b < 5 else zero for t in range(6)]
        sides.append(jnp.concatenate(tiles, axis=0))
    return jnp.concatenate(sides, axis=1)


def load_field(field_ref, values):
    rows = values[0].shape[0]
    for c in range(2):
        field_ref[c, 0:8, :] = jnp.zeros((8, values[0].shape[1]), F32)
        field_ref[c, rows : rows + 16, :] = jnp.zeros((16, values[0].shape[1]), F32)
        field_ref[c, 6 : rows + 6, :] = values[c]


def load_fold(fold_ref, tails):
    for c in range(2):
        fold_ref[c] = jnp.zeros(fold_ref.shape[1:], F32)
        for k in range(1, 7):
            fold_ref[c, 5 + k : 6 + k, :] = -tails[c][7 - k : 8 - k]


def patches(ref, start, shifted):
    tiles = []
    windows = [ref[c, start : start + 8, :] for c in range(2)]
    for t in range(6):
        tiles.append(jnp.concatenate([shifted(windows[c], t, c) for c in range(2)], axis=0))
    return jnp.concatenate(tiles, axis=0).astype(BF)


def left_sides(field_ref, fold_ref, pivot_ref, wide, pick, pick_fold, groups, rows):
    out = []
    for g in groups:
        part = dot_nt(pick, patches(field_ref, 4 * g, lambda x, t, c: roll_lanes(x, -t)))
        if 4 * g + 8 > rows + 6:
            ups = [
                jnp.broadcast_to(pivot_ref[:, c : c + 1], (8, pick.shape[1])) > wide - 1
                for c in range(2)
            ]

            def turned(x, t, c):
                return jnp.where(ups[c], roll_lanes(x, t - 1), roll_lanes(x, t + 1))

            part = part + dot_nt(pick_fold, patches(fold_ref, 4 * g - rows, turned))
        out.append(part)
    return out


def second_weights(w2_ref):
    zero = jnp.zeros(w2_ref.shape[2:], BF)

    def part(places, taps):
        rows = []
        for dr, shift in places:
            for dc in range(2):
                cells = []
                for a in taps:
                    for b in (2 * shift - dc, 2 * shift + 1 - dc):
                        inside = 0 <= a - dr < 5 and 0 <= b < 5
                        cells.append(w2_ref[a - dr, b] if inside else zero)
                rows.append(jnp.concatenate(cells, axis=1))
        return jnp.concatenate(rows, axis=0)

    return (
        part(((0, 0), (0, 1)), range(5)),
        part(((1, 0), (1, 1)), range(1, 6)),
        part(((0, 2), (1, 2)), range(6)),
    )


def block_weights(w_ref, shifts):
    zero = jnp.zeros(w_ref.shape[2:], F32)
    rows = []
    for dr in range(2):
        for dc in range(2):
            cells = []
            for er in range(2):
                for ec in shifts:
                    for r in range(2):
                        for c in range(2):
                            a, b = 2 * er + r - dr, 2 * ec + c - dc
                            inside = 0 <= a < 3 and 0 <= b < 3
                            cells.append(w_ref[a, b].astype(F32) if inside else zero)
            rows.append(jnp.concatenate(cells, axis=1))
    return rows


def edge_tile(values, blocks):
    lane = iota(values[0].shape, 1) >> 4
    tile = jnp.zeros(values[0].shape, F32)
    for value, block in zip(values, blocks):
        tile = jnp.where(lane == block, roll_lanes(value, 8 + 16 * block), tile)
    return tile


def mask_body(*refs, small):
    vel_hbm, land_hbm = refs[:2]
    own_ref, pay_ref = refs[2 + small : 4 + small]
    vel_ref, land_ref, sems = refs[4 + 2 * small :]
    moves = [(vel_hbm, vel_ref), (land_hbm, land_ref)]
    moves += list(zip(refs[2 : 2 + small], refs[4 + small : 4 + 2 * small]))
    copies = [pltpu.make_async_copy(a, b, sems.at[k]) for k, (a, b) in enumerate(moves)]
    for copy in copies:
        copy.start()
    for copy in copies[:2]:
        copy.wait()
    land = land_ref[...].astype(F32)
    own = [vel_ref[c].astype(F32) * land for c in range(2)]
    for c in range(2):
        own_ref[c] = own[c].astype(BF)
    rows = land.shape[0]
    tiles = [own[c][rows - 8 :] for c in range(2)]
    cuts = [own[c][k : k + 8] for c in range(2) for k in range(0, rows, 8)]
    tiles.append(edge_tile(cuts, range(len(cuts))))
    pay_ref[...] = jnp.concatenate(tiles, axis=0).astype(BF)
    for copy in copies[2:]:
        copy.wait()


def pair_body(pay_ref, far_ref, both_ref):
    far = far_ref[...].astype(F32)
    half = far.shape[1] // 32
    tile = edge_tile([far[0:8], far[8:16]], (half - 1, 2 * half - 1))
    own = pay_ref[...].astype(F32)[16:24]
    both_ref[...] = jnp.concatenate([own, tile], axis=0).astype(BF)


def pack_first(w1_ref, wide_ref, w1_out):
    wide_ref[...] = jnp.zeros_like(wide_ref)
    for t in range(5):
        for a in range(5):
            value = w1_ref[a, t].astype(F32)
            for c in range(2):
                wide_ref[t, c, a : a + 1, :] = value[c : c + 1]
    for t in range(5):
        base = [wide_ref[t, c] for c in range(2)]
        for row in range(4):
            both = [pltpu.roll(x, row, axis=0) if row else x for x in base]
            w1_out[row, t] = jnp.concatenate(both, axis=0).astype(BF)


def first_layer(lefts, f_ref, w1_ref, bias, start=0):
    stacked = jnp.concatenate(lefts, axis=0).astype(BF)
    size = lefts[0].shape[0]
    for row in range(4):
        res = dot(stacked, first_weights(w1_ref, row))
        res = jnp.maximum(res + bias, 0.0).astype(BF)
        for g in range(len(lefts)):
            f_ref[row % 2, 2 * (start + g) + row // 2] = res[size * g : size * g + size]


def second_layer(f_ref, right, acc_ref, lo, count):
    size = f_ref.shape[2]
    left = jnp.concatenate(
        [
            f_ref[a % 2, lo + a // 2 : lo + a // 2 + count].reshape(count * size, 256)
            for a in range(6)
        ],
        axis=1,
    )
    rows = count * size
    for dr, cut in enumerate((left[:, : 5 * 256], left[:, 256:])):
        res = dot_nt(cut, right[dr])
        lanes = slice(128 * dr, 128 * dr + 128)
        for shift in range(2):
            acc_ref[shift, 0:rows, lanes] = res[:, 128 * shift : 128 * shift + 128]
    acc_ref[2, 0:rows, :] = dot_nt(left, right[2])


def shifted_sum(acc_ref, at, size, bias):
    parts = [acc_ref[k, at + k : at + k + size, :] for k in range(acc_ref.shape[0])]
    total = parts[0]
    for part in parts[1:]:
        total = total + part
    return jnp.maximum(total + bias, 0.0)


def inner_second(f_ref, right, bias, acc_ref, sec_ref, start, count):
    chunks = acc_ref.shape[0]
    step = count // chunks
    for k in range(chunks):
        second_layer(f_ref, right, acc_ref.at[k], start + k * step, step)
        for p in range(step):
            at = (start + k * step + p) * LINE
            sec_ref[at : at + 64, :] = shifted_sum(acc_ref.at[k], 64 * p, 64, bias).astype(BF)


def inner_picks(cols):
    lane = iota((64, cols), 1)
    slot = iota((64, cols), 0)
    fold = lax.rem(2 * cols + 5 - 2 * slot, cols)
    return (lane == 2 * slot - 6).astype(BF), (lane == fold).astype(BF)


def local_first(own_ref, w1_ref, b1_ref, w2_hbm, f, w1_out, w2_out, field, wide, sem):
    copy = pltpu.make_async_copy(w2_hbm, w2_out, sem)
    copy.start()
    pack_first(w1_ref, wide, w1_out)
    rows = own_ref.shape[1]
    cols = own_ref.shape[2]
    load_field(field, [own_ref[c].astype(F32) for c in range(2)])
    pick, _ = inner_picks(cols)
    lefts = left_sides(field, None, None, 0, pick, None, range((rows - 2) // 4 + 1), rows)
    first_layer(lefts, f, w1_out, jnp.concatenate([b1_ref[...]] * 2, axis=1))
    copy.wait()


def early_body(own_ref, w1_ref, b1_ref, w2_hbm, pay_in, pay, f, w1_out, w2_out, field, wide, sem):
    @pl.when(lax.axis_index("lon") == 0)
    def _():
        local_first(own_ref, w1_ref, b1_ref, w2_hbm, f, w1_out, w2_out, field, wide, sem)


def south_body(
    own_ref, w1_ref, b1_ref, w2_hbm, b2_ref, f_in, w1_in, w2_in, sec, f, w1_out, w2_out,
    field, acc, wide, sem,
):
    @pl.when(lax.axis_index("lon") != 0)
    def _():
        local_first(own_ref, w1_ref, b1_ref, w2_hbm, f, w1_out, w2_out, field, wide, sem)

    bias2 = jnp.concatenate([b2_ref[...]] * 4, axis=1)
    inner_second(f, second_weights(w2_out), bias2, acc, sec, 0, SPLIT)


def north_body(
    pivot_ref, own_ref, far_ref, w1_ref, b1_ref, w2_ref, b2_ref, w3_ref, w4_ref, sec_in,
    f_in, sec, w3_out, w4_out, sel_out, f, field, fold, acc, *, lon_count,
):
    bias1 = jnp.concatenate([b1_ref[...]] * 2, axis=1)
    bias2 = jnp.concatenate([b2_ref[...]] * 4, axis=1)
    rows = own_ref.shape[1]
    cols = own_ref.shape[2]
    blocks = block_weights(w3_ref, (0,)) + block_weights(w3_ref, (1,))
    w3_out[...] = jnp.concatenate(blocks, axis=0).astype(BF)
    tiny = block_weights(w4_ref, (0, 1))
    blank = jnp.zeros((4, tiny[0].shape[1]), F32)
    order = [tiny[0], tiny[2], blank, tiny[1], tiny[3], blank]
    w4_out[...] = jnp.concatenate(order, axis=0).astype(BF)
    src = iota((256, 256), 0)
    want = 2 * (src & 127) + (src >> 7)
    sel_out[...] = (iota((256, 256), 1) == want).astype(BF)
    load_field(field, [own_ref[c].astype(F32) for c in range(2)])
    far = far_ref[...].astype(F32)
    load_fold(fold, [far[8 * c : 8 * c + 8] for c in range(2)])
    pick, pick_fold = inner_picks(cols)
    groups = range((rows - 2) // 4 + 1, (rows + 8) // 4)
    lefts = left_sides(field, fold, pivot_ref, lon_count * cols, pick, pick_fold, groups, rows)
    first_layer(lefts, f, w1_ref, bias1, groups[0])
    count = (rows + 4) // 2 - SPLIT
    inner_second(f, second_weights(w2_ref), bias2, acc, sec, SPLIT, count)


def last_body(
    pivot_ref, lon_ref, b4_ref, vel_ref, land_ref, own_ref, pay_ref, far_ref, near_a_ref, near_b_ref,
    w1_ref, b1_ref, w2_ref, b2_ref, w3_ref, b3_ref, w4_ref, sel_ref, sec_in,
    out_ref, field, fold, f, acc, strip, accs, acc3, third, spill, tend, *, lon_count,
):
    rows = own_ref.shape[1]
    cols = own_ref.shape[2]
    bias1 = jnp.concatenate([b1_ref[...]] * 2, axis=1)
    bias2 = jnp.concatenate([b2_ref[...]] * 4, axis=1)
    bias3 = jnp.concatenate([b3_ref[...]] * 4, axis=1)
    groups = (rows + 8) // 4
    pairs = (rows + 4) // 2

    lon = jnp.broadcast_to(lon_ref[...], (16, cols))
    even = (lon & 1) == 0
    own = own_ref[...].astype(F32)
    far = far_ref[...].astype(F32)
    wrap = jnp.concatenate([far[16:24], pay_ref[...].astype(F32)[16:24]], axis=0)
    near_a = near_a_ref[...].astype(F32)
    near_b = near_b_ref[...].astype(F32)
    west = jnp.where(lon == 0, wrap, jnp.where(even, near_b, near_a))
    east = jnp.where(lon == lon_count - 1, wrap, jnp.where(even, near_a, near_b))
    lane = iota((8, cols), 1)
    half = cols // 2

    def around(mid, after, before, block):
        outer = jnp.where(
            lane < half // 2,
            roll_lanes(after, -16 * block - 8),
            roll_lanes(before, half - 8 - 16 * block),
        )
        inner = jnp.where(lane < half + half // 2, roll_lanes(mid, half), mid)
        return jnp.where(lane < half, outer, inner)

    wide = []
    tails = []
    for c in range(2):
        parts = []
        for k in range(rows // 8):
            block = c * (rows // 8) + k
            parts.append(around(own[c, 8 * k : 8 * k + 8], east[0:8], west[0:8], block))
        wide.append(jnp.concatenate(parts, axis=0))
        tails.append(around(far[8 * c : 8 * c + 8], west[8:16], east[8:16], block))
    load_field(field, wide)
    load_fold(fold, tails)
    slot = iota((2 * EDGE, cols), 0)
    lane = iota((2 * EDGE, cols), 1)
    low = slot < EDGE
    pair = jnp.where(low, slot, slot + (cols // 2 - 4 - EDGE))
    start = 2 * pair - 6 + jnp.where(low, cols // 2, 0)
    pick = (lane == lax.rem(start + cols, cols)).astype(BF)
    start = cols + 5 - 2 * pair + jnp.where(low, 0, cols // 2)
    pick_fold = (lane == lax.rem(start + cols, cols)).astype(BF)
    lefts = left_sides(
        field, fold, pivot_ref, lon_count * cols, pick, pick_fold, range(groups), rows
    )
    first_layer(lefts, f, w1_ref, bias1)
    second_layer(f, second_weights(w2_ref), acc, 0, pairs)
    pairs3 = pairs - 1
    right = w3_ref[...]
    for part, (lo, hi) in enumerate(((0, pairs3),)):
        base, size = lo * LINE, (hi - lo) * LINE
        left = [sec_in[base + at : base + at + size, :] for at in (0, LINE)]
        res = dot_nt(jnp.concatenate(left, axis=1), right)
        for shift in range(2):
            acc3[part, shift, 0:size, :] = res[:, 128 * shift : 128 * shift + 128]
        for shift in range(2):
            value = shifted_sum(acc3.at[part], shift, size, bias3)
            third[shift, base : base + size, :] = value.astype(BF)

    strip[...] = shifted_sum(acc, 0, 2 * EDGE * pairs, bias2).astype(BF)
    size = 2 * EDGE * pairs3
    res = dot_nt(jnp.concatenate([strip[0:size], strip[2 * EDGE :]], axis=1), w3_ref[...])
    for shift in range(2):
        accs[shift, 0:size, :] = res[:, 128 * shift : 128 * shift + 128]
    for shift in range(2):
        edge = shifted_sum(accs, shift, size, bias3)
        first = edge.astype(BF)
        last = pltpu.roll(edge, 4, axis=0).astype(BF)
        for k in range(pairs3):
            at = k * LINE
            third[shift, at : at + 4, :] = first[2 * EDGE * k : 2 * EDGE * k + 4]
            third[shift, at + 60 : at + 64, :] = last[2 * EDGE * k + 12 : 2 * EDGE * k + 16]

    pairs4 = pairs - 2
    right = w4_ref[...]
    tiles = []
    for lo in (0, pairs4 // 2):
        left = jnp.concatenate(
            [
                jnp.concatenate(
                    [
                        third[shift, k * LINE : k * LINE + 64, :]
                        for k in range(lo + up, lo + up + pairs4 // 2)
                    ],
                    axis=0,
                )
                for up in range(2)
                for shift in range(2)
            ],
            axis=1,
        )
        res = dot_nt(right, left)
        tiles += [res[:, 128 * t : 128 * t + 128] for t in range(pairs4 // 4)]
    stack = jnp.concatenate(
        [jnp.concatenate([x[8 * dc : 8 * dc + 8] for x in tiles], axis=0) for dc in range(2)], axis=1
    )
    upper = stack.astype(BF)
    lower = (stack - upper.astype(F32)).astype(BF)
    res = dot(jnp.concatenate([upper, lower], axis=0), sel_ref[...])
    count = 8 * len(tiles)
    res = res[:count] + res[count:]
    for k in range(2):
        spill[k] = res[:, 128 * k : 128 * k + 128]
    for c in range(2):
        for dr in range(2):
            for k in range(2):
                tend[c, pl.ds(2 * k + dr, pairs4 // 2, stride=4), :] = spill[
                    k, pl.ds(dr * 2 + c, pairs4 // 2, stride=8), :
                ]
    land = land_ref[...].astype(F32)
    for c in range(2):
        bias4 = jnp.broadcast_to(b4_ref[:, c : c + 1], (1, cols))
        total = vel_ref[c].astype(F32) + (tend[c] + bias4)
        out_ref[c] = (land * total).astype(BF)


def call(fn, ins, outs, scratch, flops=0, aliases=None, far_ins=()):
    vmem = pl.BlockSpec(memory_space=pltpu.VMEM)
    hbm = pl.BlockSpec(memory_space=pltpu.HBM)
    specs = [vmem] * len(ins)
    ins = list(ins)
    for k in far_ins:
        specs[k] = hbm
        ins[k] = pltpu.with_memory_space_constraint(ins[k], pltpu.HBM)
    return pl.pallas_call(
        fn,
        out_shape=outs,
        in_specs=specs,
        out_specs=[vmem] * len(outs),
        scratch_shapes=scratch,
        input_output_aliases=aliases or {},
        cost_estimate=pl.CostEstimate(flops=flops, bytes_accessed=1 << 20, transcendentals=0),
        compiler_params=pltpu.CompilerParams(
            vmem_limit_bytes=32 << 20
        ),
    )(*ins)


def step(velocity, land_sea, fold_pivot, w1, b1, w2, b2, w3, b3, w4, b4):
    rows = velocity.shape[2]
    cols = velocity.shape[3]
    n = lax.axis_size("lon")
    lon = jnp.full((1, 1), lax.axis_index("lon"), jnp.int32)
    vel = velocity.reshape(2, rows, cols)
    land = land_sea.reshape(rows, cols)
    w2, w3, w4 = (jnp.swapaxes(w, 2, 3) for w in (w2, w3, w4))
    b1, b2, b3, b4, fold_pivot = (x[None] for x in (b1, b2, b3, b4, fold_pivot))
    shape = jax.ShapeDtypeStruct
    scratch = pltpu.VMEM
    sems = pltpu.SemaphoreType.DMA
    near = [w1, b1, b2, b3, b4, fold_pivot]
    own, pay, w1, b1, b2, b3, b4, fold_pivot = call(
        functools.partial(mask_body, small=len(near)),
        [vel, land] + near,
        [shape(vel.shape, BF), shape((24, cols), BF)] + [shape(x.shape, x.dtype) for x in near],
        [scratch(vel.shape, BF), scratch(land.shape, jnp.int32), sems((2 + len(near),))],
        far_ins=range(2 + len(near)),
    )
    mirror = [(i, n - 1 - i) for i in range(n)]
    pairs_a = [(i, i ^ 1) for i in range(n)]
    levels = lax.axis_size("lev")
    pairs_b = []
    for level in range(levels):
        for k in range(1, n // 2):
            low, high = (2 * k - 1) * levels + level, 2 * k * levels + level
            pairs_b += [(low, high), (high, low)]
        for end in (0, n - 1):
            pairs_b.append((end * levels + level, end * levels + (level + 1) % levels))
    groups = (rows + 8) // 4
    pairs = (rows + 4) // 2
    sec_shape = shape((pairs * LINE, 256), BF)
    f_shape = shape((2, 2 * groups, 64, 256), BF)
    packed = (4, 5, 16, w1.shape[3])
    field = scratch((2, rows + 16, cols), F32)
    fold = scratch((2, 16, cols), F32)
    made = [f_shape, shape(packed, BF), shape(w2.shape, BF)]
    wide = scratch((5, 2, 8, w1.shape[3]), F32)
    pay, f, w1_wide, w2_near = call(
        early_body,
        [own, w1, b1, w2, pay],
        [shape(pay.shape, BF)] + made,
        [field, wide, sems(())],
        far_ins=(3,),
        aliases={4: 0},
    )
    far = lax.ppermute(pay, "lon", mirror)
    sec, f, w1_wide, w2 = call(
        south_body,
        [own, w1, b1, w2, b2, f, w1_wide, w2_near],
        [sec_shape] + made,
        [field, scratch((1, 3, 64 * SPLIT + 8, 256), F32), wide, sems(())],
        flops=2 * 64 * SPLIT * 256 * 4608,
        far_ins=(3,),
        aliases={5: 1, 6: 2, 7: 3},
    )
    (both,) = call(pair_body, [pay, far], [shape((16, cols), BF)], [])
    near_a = lax.ppermute(both, "lon", pairs_a)
    near_b = lax.ppermute(both, ("lon", "lev"), pairs_b)
    sec, w3_wide, w4_wide, sel, _ = call(
        functools.partial(north_body, lon_count=n),
        [fold_pivot, own, far, w1_wide, b1, w2, b2, w3, w4, sec, f],
        [sec_shape, shape((256, 512), BF), shape((16, 512), BF), shape((256, 256), BF), f_shape],
        [field, fold, scratch((1, 3, 64 * (pairs - SPLIT) + 8, 256), F32)],
        flops=2 * 64 * (pairs - SPLIT) * 256 * 4608,
        aliases={9: 0, 10: 4},
    )
    (out,) = call(
        functools.partial(last_body, lon_count=n),
        [fold_pivot, lon, b4, vel, land, own, pay, far, near_a, near_b]
        + [w1_wide, b1, w2, b2, w3_wide, b3, w4_wide, sel, sec],
        [shape((2, rows, cols), BF)],
        [
            field,
            fold,
            scratch((2, 2 * groups, 2 * EDGE, 256), BF),
            scratch((3, 2 * pairs * EDGE + 8, 256), F32),
            scratch((2 * pairs * EDGE, 256), BF),
            scratch((2, 2 * pairs * EDGE + 8, 128), F32),
            scratch((1, 2, pairs * LINE + 16, 128), F32),
            scratch((2, pairs * LINE, 128), BF),
            scratch((2, 64, 128), F32),
            scratch((2, rows, cols), F32),
        ],
        flops=2 * 64 * pairs * 256 * 1024,
    )
    return out.reshape(velocity.shape)


def solution(mesh):
    in_specs = (
        P(None, ("members", "lev"), None, "lon"),
        P(("members", "lev"), None, "lon"),
    ) + (P(),) * 9
    out_specs = P(None, ("members", "lev"), None, "lon")
    return jax.shard_map(step, mesh=mesh, in_specs=in_specs, out_specs=out_specs, check_vma=False)
```
